512 devices in a mesh: mem: 64 (over y, z_lo, core), band: 8 (over x, z_hi).
Axes of the slice: x: 4, y: 8, z: 8 (z_hi: 2, z_lo: 4; z = z_hi * 4 + z_lo), core: 2. Of those that a mesh axis runs over, the one named last changes fastest.
Arguments:
- ensemble: bfloat16 [64, 12, 128, 512], P('mem', None, 'band'), may hold values from -6 to 6
- alpha: float32 [64, 12, 128, 512], P('mem', None, 'band'), may hold values from -6 to 6
- lat_lower: int32 [384], P('band'), may hold values from -1 to 15, as said below
- lat_weight: float32 [384], P('band'), may hold values from 0 to 1
- background: float32 [12, 512, 1152], P(None, ('band', 'mem')), may hold values from -6 to 6
- obs_cell: int32 [512, 256], P(('band', 'mem')), may hold values from 0 to 1151
- obs_value: float32 [12, 512, 256], P(None, ('band', 'mem')), may hold values from -6 to 6
- obs_precision: float32 [512, 256], P(('band', 'mem')), may hold values from 1 to 10
Outputs:
- advected: float32 [12, 512, 1152], P(None, ('band', 'mem'))
- gradient: float32 [64, 12, 128, 512], P('mem', None, 'band')
The draws below stay inside these ranges and needn't reach their ends.
Inputs may be any that keep to these rules, and one draw needn't show every extreme that they name: `lat_lower`: fine rows of the first band use lower rows from 0, those of the last band up to 14 of their band, so that their upper row reaches 15; other bands reach -1 and 15. `obs_cell`: the cell is r * 24 + c for fine row r and column c within the tile.
All inputs are finite; a program needn't handle non-finite values.
Results may differ from the reference program's by a relative error of at most 0.0004.
Values sent between devices are 32-bit elements; how exact they have to be, the bound alone decides.
No kernel may reach another device: no remote copies, remote signals or barrier semaphores. Data moves between devices by JAX's collectives and lax.ppermute only.
A program may use at most 64 MiB of HBM per device.

```python
import math
import jax
import jax.numpy as jnp
from jax import lax

LEV = 12
CLAT_B = 16
NOBS = 256
MEMBERS = 64
CLAT = 128
CLON = 512
FLAT_B = 48
FLON_T = 24
FLAT = 384
FLON = 1536
TILES = 512
TILE_CELLS = 1152
N_MEM = 64
N_BAND = 8


def draw_lat_lower(key, part):
    fine_index = jnp.arange(FLAT, dtype=jnp.int32)
    inner = fine_index % FLAT_B
    band_index = fine_index // FLAT_B
    jitter = jax.random.randint(key, (FLAT,), 0, 2, dtype=jnp.int32)
    jitter = jnp.where(inner == 0, 0, jnp.where(inner == FLAT_B - 1, 1, jitter))
    lower_row = inner * CLAT_B // FLAT_B - 1 + jitter
    lower_row = jnp.where(band_index == 0, jnp.maximum(lower_row, 0), lower_row)
    lower_row = jnp.where(band_index == FLAT // FLAT_B - 1, jnp.minimum(lower_row, CLAT_B - 2), lower_row)
    return lower_row.astype(jnp.int32)


def touch_ends(values, stream_key, smallest, high):
    longest = values.shape.index(max(values.shape))
    spots = []
    for shift in (0, 1):
        where = [jax.random.randint(jax.random.fold_in(stream_key, axis), (), 0, length) for axis, length in enumerate(values.shape)]
        where[longest] = (where[longest] + shift) % values.shape[longest]
        spots.append(tuple(where))
    return values.at[spots[0]].set(smallest).at[spots[1]].set(high)


def level_of(key, extent, shards, least, largest):
    def one(axis_at, parts):
        steps = jax.random.uniform(jax.random.fold_in(jax.random.fold_in(key, 6), axis_at), (parts,), jnp.float32, least / len(shards), largest / len(shards))
        return jnp.repeat(jnp.exp(steps), extent[axis_at] // parts).reshape((-1,) + (1,) * (len(extent) - axis_at - 1))

    level = one(*shards[0])
    for cut in shards[1:]:
        level = level * one(*cut)
    return level


def centred(stream_key, shape, scale, most, cuts=(), kind=jnp.bfloat16):
    result = scale * jax.random.normal(stream_key, shape, jnp.float32)
    if cuts:
        result = result * level_of(stream_key, shape, cuts, -0.22, 0.18)
    return jnp.clip(result, -most, most).astype(kind)


def setup_inputs(seed: int = 0) -> dict:
    key_of = jax.random.split(jax.random.key(seed), 9)
    ensemble = centred(key_of[0], (MEMBERS, LEV, CLAT, CLON), 1.0, 6.0, ((0, 64), (2, 8)))
    alpha = centred(key_of[1], (MEMBERS, LEV, CLAT, CLON), 1.0, 6.0, ((0, 64), (2, 8)), jnp.float32)
    lat_lower = draw_lat_lower(jax.random.fold_in(key_of[8], 71), 0)
    lat_weight = jnp.clip(1.0 * jax.random.uniform(key_of[3], (FLAT,), jnp.float32) ** level_of(key_of[3], (FLAT,), ((0, 8),), -0.2, 0.2), 0.0, 1.0)
    background = centred(key_of[4], (LEV, TILES, TILE_CELLS), 1.0, 6.0, ((1, 512),), jnp.float32)
    obs_cell = touch_ends(jax.random.randint(key_of[5], (TILES, NOBS), 0, TILE_CELLS), jax.random.fold_in(key_of[5], 1), 0, TILE_CELLS - 1).astype(jnp.int32)
    obs_value = centred(key_of[6], (LEV, TILES, NOBS), 1.0, 6.0, ((1, 512),), jnp.float32)
    obs_precision = jnp.clip(jnp.exp(math.log(10.0) - 2.3025851 * jax.random.uniform(key_of[7], (TILES, NOBS), jnp.float32) ** level_of(key_of[7], (TILES, NOBS), ((0, 512),), -0.2, 0.2)), 1.0, 10.0)
    return {"ensemble": ensemble, "alpha": alpha, "lat_lower": lat_lower, "lat_weight": lat_weight, "background": background, "obs_cell": obs_cell, "obs_value": obs_value, "obs_precision": obs_precision}


advect_rate = 0.25
highest = lax.Precision.HIGHEST

def smooth_field(grid_field):
    padded = jnp.pad(grid_field, ((0, 0), (0, 0), (1, 1), (0, 0)))
    grid_field = 0.25 * padded[:, :, :-2] + 0.5 * padded[:, :, 1:-1] + 0.25 * padded[:, :, 2:]
    return 0.25 * jnp.roll(grid_field, 1, 3) + 0.5 * grid_field + 0.25 * jnp.roll(grid_field, -1, 3)

def latitude_table(lat_lower, lat_weight):
    fine_index = jnp.arange(FLAT, dtype=jnp.int32)
    lower_row = fine_index // FLAT_B * CLAT_B + lat_lower
    coarse = jnp.arange(CLAT, dtype=jnp.int32)
    weight = lat_weight[:, None]
    return (1.0 - weight) * (coarse[None, :] == lower_row[:, None]) + weight * (coarse[None, :] == lower_row[:, None] + 1)

def longitude_table(coarse_cols, fine_cols):
    fine_ratio = fine_cols // coarse_cols
    fine_index = jnp.arange(fine_cols, dtype=jnp.int32)
    numerator = 2 * fine_index + 1 + fine_ratio
    upper_col = numerator // (2 * fine_ratio)
    fraction = (numerator % (2 * fine_ratio)).astype(jnp.float32) / (2 * fine_ratio)
    coarse = jnp.arange(coarse_cols, dtype=jnp.int32)[:, None]
    low_col = (upper_col - 1) % coarse_cols
    high_col = upper_col % coarse_cols
    return (1.0 - fraction)[None, :] * (coarse == low_col[None, :]) + fraction[None, :] * (coarse == high_col[None, :])

def reference(ensemble, alpha, lat_lower, lat_weight, background, obs_cell, obs_value, obs_precision):
    member_scale = 1.0 / math.sqrt(MEMBERS - 1)
    members_f = ensemble.astype(jnp.float32)
    increment = lax.optimization_barrier(jnp.sum(smooth_field(alpha) * members_f, axis=0)) * member_scale
    lat_table = latitude_table(lat_lower, lat_weight)
    lon_table = longitude_table(CLON, FLON)
    fine_grid = background.reshape(LEV, N_BAND, N_MEM, FLAT_B, FLON_T).transpose(0, 1, 3, 2, 4).reshape(LEV, FLAT, FLON)
    indices = jnp.broadcast_to(obs_cell[None], (LEV, TILES, NOBS))

    def fine_model(incr):
        lat_rows = jnp.einsum('ik,lkc->lic', lat_table, incr, precision=highest)
        fine_incr = jnp.einsum('lic,cj->lij', lat_rows, lon_table, precision=highest)
        fine_state = fine_grid + fine_incr
        lon_slope = 0.5 * (jnp.roll(fine_state, -1, 2) - jnp.roll(fine_state, 1, 2))
        moved = fine_state - advect_rate * fine_state * lon_slope
        return moved.reshape(LEV, N_BAND, FLAT_B, N_MEM, FLON_T).transpose(0, 1, 3, 2, 4).reshape(LEV, TILES, TILE_CELLS)

    def observed_of(incr):
        return jnp.take_along_axis(fine_model(incr), indices, axis=2)
    advected = fine_model(increment)
    observed, pullback = jax.vjp(observed_of, increment)
    weighted = obs_precision[None] * (observed - obs_value)
    coarse_gradient = pullback(weighted)[0]
    gradient = smooth_field(members_f * coarse_gradient[None] * member_scale)
    return (advected, gradient)
```

```python
import functools
import math

import jax
import jax.numpy as jnp
from jax import lax
from jax.experimental import pallas as pl
from jax.experimental.pallas import tpu as pltpu
from jax.sharding import PartitionSpec as P

LEV = 12
LPAD = 16
ROWS = 16
COLS = 512
GROUPS = 64
BLOCK = COLS // GROUPS
FRAME = BLOCK + 2
FINE_R = 48
FINE_C = 24
NOBS = 256
Q = LEV * (ROWS + 2)
TILES_PER = 17
CHUNK = TILES_PER * 128
MAIN = LEV * ROWS

advect_rate = 0.25
highest = lax.Precision.HIGHEST


def lon_smooth(x):
    axis = x.ndim - 1
    return 0.25 * pltpu.roll(x, 1, axis) + 0.5 * x + 0.25 * pltpu.roll(x, COLS - 1, axis)


def interp(j):
    n = 2 * j + 4
    return n // 6, (n % 6) / 6.0


def product_kernel(scale, alpha_ref, ens_ref, prev_ref, next_ref, out_ref, pad, x_ref, xt_lo, xt_hi, flat):
    pad[:, 8:24, :] = alpha_ref[...]
    pad[:, 7, :] = prev_ref[1]
    pad[:, 24, :] = next_ref[0]
    body = 0.25 * pad[:, 7:23, :] + 0.5 * alpha_ref[...] + 0.25 * pad[:, 9:25, :]
    body = lon_smooth(body) * (ens_ref[...].astype(jnp.float32) * scale)
    top = 0.25 * prev_ref[0] + 0.5 * prev_ref[1] + 0.25 * alpha_ref[:, 0, :]
    low = 0.25 * alpha_ref[:, ROWS - 1, :] + 0.5 * next_ref[0] + 0.25 * next_ref[1]
    x_ref[:MAIN, :] = body.reshape(MAIN, COLS)
    x_ref[MAIN : MAIN + LEV, :] = lon_smooth(top) * (prev_ref[2] * scale)
    x_ref[MAIN + LEV : Q, :] = lon_smooth(low) * (next_ref[2] * scale)
    x_ref[Q:, :] = jnp.zeros((256 - Q, COLS), jnp.float32)
    for half, xt in enumerate((xt_lo, xt_hi)):
        xt[8 : 8 + COLS, :] = x_ref[128 * half : 128 * (half + 1), :].T
        xt[7:8, :] = xt[7 + COLS : 8 + COLS, :]
        xt[8 + COLS : 9 + COLS, :] = xt[8:9, :]
    flat[:, FRAME * Q :] = jnp.zeros((GROUPS, CHUNK - FRAME * Q), jnp.float32)
    for c in range(FRAME):
        rows = pl.ds(7 + c, GROUPS, stride=BLOCK)
        flat[:, c * Q : c * Q + 128] = xt_lo[rows, :]
        flat[:, c * Q + 128 : (c + 1) * Q] = xt_hi[rows, :][:, : Q - 128]
    for t in range(TILES_PER):
        out_ref[pl.ds(t, GROUPS, stride=TILES_PER), :] = flat[:, 128 * t : 128 * (t + 1)]


def tile_kernel(g_ref, bg_ref, lower_ref, weight_ref, row_ref, col_ref, val_ref, prec_ref,
                adv_ref, own_ref, up_ref, down_ref, flat):
    for t in range(TILES_PER):
        part = g_ref[pl.ds(t, GROUPS, stride=TILES_PER), :]
        flat[0:1, 128 * t : 128 * (t + 1)] = jnp.sum(part, axis=0, keepdims=True)
    q = lax.broadcasted_iota(jnp.int32, (1, Q), 1)
    spot = jnp.where(q < MAIN, (q & 15) + 1, jnp.where(q < MAIN + LEV, 0, ROWS + 1))
    level = jnp.where(q < MAIN, q >> 4, jnp.where(q < MAIN + LEV, q - MAIN, q - MAIN - LEV))
    mask = lax.broadcasted_iota(jnp.int32, (LPAD, Q), 0) == level
    low = lower_ref[...] + 1
    weight = weight_ref[...]

    def table(place):
        return jnp.where(place == low, 1.0 - weight, 0.0) + jnp.where(place == low + 1, weight, 0.0)

    lat = table(spot)
    spread = [jnp.where(mask, flat[0:1, c * Q : (c + 1) * Q], 0.0) for c in range(FRAME)]
    lat_rows = lax.dot_general(jnp.concatenate(spread, axis=0), lat, (((1,), (1,)), ((), ())), precision=highest,
                               preferred_element_type=jnp.float32).reshape(FRAME, LPAD, FINE_R)
    state = []
    for j in range(-1, FINE_C + 1):
        lo, f = interp(j)
        state.append((1.0 - f) * lat_rows[lo] + f * lat_rows[lo + 1] + bg_ref[j + 1])
    slope = [0.5 * (state[j + 2] - state[j]) for j in range(FINE_C)]
    model = [state[j + 1] - advect_rate * state[j + 1] * slope[j] for j in range(FINE_C)]
    for j in range(FINE_C):
        adv_ref[j] = model[j]
    pick_row = (lax.broadcasted_iota(jnp.int32, (FINE_R, NOBS), 0) == row_ref[...]).astype(jnp.float32)
    pick_col = [(col_ref[...] == j).astype(jnp.float32) for j in range(FINE_C)]
    seen = jnp.dot(jnp.concatenate(model, axis=0), pick_row, precision=highest,
                   preferred_element_type=jnp.float32).reshape(FINE_C, LPAD, NOBS)
    observed = sum(pick_col[j] * seen[j] for j in range(FINE_C))
    weighted = prec_ref[...] * (observed - val_ref[...])
    back = jnp.concatenate([pick_col[j] * weighted for j in range(FINE_C)], axis=0)
    cot = lax.dot_general(back, pick_row, (((1,), (1,)), ((), ())), precision=highest,
                          preferred_element_type=jnp.float32).reshape(FINE_C, LPAD, FINE_R)
    half_rate = 0.5 * advect_rate
    flux = [half_rate * state[j + 1] * cot[j] for j in range(FINE_C)]
    total = [None] * FRAME
    for j in range(-1, FINE_C + 1):
        adj = None
        if 0 <= j < FINE_C:
            adj = cot[j] - advect_rate * cot[j] * slope[j]
        if j + 1 < FINE_C:
            adj = flux[j + 1] if adj is None else adj + flux[j + 1]
        if j - 1 >= 0:
            adj = -flux[j - 1] if adj is None else adj - flux[j - 1]
        lo, f = interp(j)
        for c, w in ((lo, 1.0 - f), (lo + 1, f)):
            if w:
                total[c] = w * adj if total[c] is None else total[c] + w * adj
    coarse = jnp.concatenate(total, axis=0)
    for place, ref in ((spot, own_ref), (spot + ROWS, up_ref), (spot - ROWS, down_ref)):
        lat = table(place)
        wide = jnp.dot(coarse, lat, precision=highest, preferred_element_type=jnp.float32).reshape(FRAME, LPAD, Q)
        for c in range(FRAME):
            flat[0:1, c * Q : (c + 1) * Q] = jnp.sum(jnp.where(mask, wide[c], 0.0), axis=0, keepdims=True)
        for t in range(TILES_PER):
            ref[t : t + 1, :] = flat[0:1, 128 * t : 128 * (t + 1)]


def share_kernel(own_ref, prev_ref, next_ref, out_ref):
    total = own_ref[...] + prev_ref[...] + next_ref[...]
    for m in range(GROUPS):
        out_ref[TILES_PER * m : TILES_PER * (m + 1), :] = total


def gradient_kernel(scale, g_ref, ens_ref, prev_ref, next_ref, out_ref, pad, xt_lo, xt_hi, flat):
    for t in range(TILES_PER):
        flat[:, 128 * t : 128 * (t + 1)] = g_ref[pl.ds(t, GROUPS, stride=TILES_PER), :]
    slots = [flat[:, c * Q : (c + 1) * Q] for c in range(FRAME)]
    slots[1] = slots[1] + pltpu.roll(slots[FRAME - 1], 1, 0)
    slots[BLOCK] = slots[BLOCK] + pltpu.roll(slots[0], GROUPS - 1, 0)
    for c in range(1, BLOCK + 1):
        rows = pl.ds(c - 1, GROUPS, stride=BLOCK)
        xt_lo[rows, :] = slots[c][:, :128]
        xt_hi[rows, : Q - 128] = slots[c][:, 128:]
    lo = xt_lo[...].T * scale
    hi = xt_hi[...].T * scale
    field = jnp.concatenate([lo, hi[: MAIN - 128, :]], axis=0).reshape(LEV, ROWS, COLS) * ens_ref[...].astype(jnp.float32)
    pad[:, 8:24, :] = field
    pad[:, 7, :] = hi[MAIN - 128 : MAIN - 128 + LEV, :] * prev_ref[2]
    pad[:, 24, :] = hi[MAIN - 128 + LEV : Q - 128, :] * next_ref[2]
    out_ref[...] = lon_smooth(0.25 * pad[:, 7:23, :] + 0.5 * field + 0.25 * pad[:, 9:25, :])


def call(kernel, out, scratch, *args):
    return pl.pallas_call(
        kernel,
        out_shape=out,
        in_specs=[pl.BlockSpec(memory_space=pltpu.VMEM)] * len(args),
        out_specs=jax.tree.map(lambda _: pl.BlockSpec(memory_space=pltpu.VMEM), out),
        scratch_shapes=scratch,
        compiler_params=pltpu.CompilerParams(vmem_limit_bytes=40 * 1024 * 1024),
    )(*args)


def f32(*shape):
    return jax.ShapeDtypeStruct(shape, jnp.float32)


def both_ways(up_value, down_value, axis, wrap):
    size = lax.axis_size(axis)
    up = [(i, (i + 1) % size) for i in range(size if wrap else size - 1)]
    down = [(j, i) for i, j in up]
    return lax.ppermute(up_value, axis, up), lax.ppermute(down_value, axis, down)


def exchange(flat):
    parts = lax.all_to_all(flat.reshape(GROUPS, 1, CHUNK), "mem", 0, 0, tiled=True)
    return parts.reshape(GROUPS * TILES_PER, 128)


def shards(ensemble, alpha, lat_lower, lat_weight, background, obs_cell, obs_value, obs_precision):
    scale = 1.0 / math.sqrt(GROUPS - 1)
    ens = ensemble[0]
    alf = alpha[0]
    last = jnp.stack([alf[:, ROWS - 2], alf[:, ROWS - 1], ens[:, ROWS - 1].astype(jnp.float32)])
    first = jnp.stack([alf[:, 0], alf[:, 1], ens[:, 0].astype(jnp.float32)])
    before, after = both_ways(last, first, "band", False)

    grid = background.reshape(LEV, FINE_R, FINE_C).transpose(2, 0, 1)
    left, right = both_ways(grid[FINE_C - 1], grid[0], "mem", True)
    wide = jnp.concatenate([left[None], grid, right[None]], axis=0)
    wide = jnp.pad(wide, ((0, 0), (0, LPAD - LEV), (0, 0)))
    value = jnp.pad(obs_value[:, 0, :], ((0, LPAD - LEV), (0, 0)))

    vmem = pltpu.VMEM
    packed = call(
        functools.partial(product_kernel, scale),
        f32(GROUPS * TILES_PER, 128),
        [vmem((LEV, 32, COLS), jnp.float32), vmem((256, COLS), jnp.float32), vmem((COLS + 16, 128), jnp.float32),
         vmem((COLS + 16, 128), jnp.float32), vmem((GROUPS, CHUNK), jnp.float32)],
        alf, ens, before, after,
    )
    gathered = exchange(packed)
    moved, own, up, down = call(
        tile_kernel,
        (f32(FINE_C, LPAD, FINE_R), f32(TILES_PER, 128), f32(TILES_PER, 128), f32(TILES_PER, 128)),
        [vmem((8, CHUNK), jnp.float32)],
        gathered, wide, lat_lower[:, None], lat_weight[:, None], obs_cell // FINE_C, obs_cell % FINE_C, value, obs_precision,
    )
    from_prev, from_next = both_ways(up, down, "band", False)
    shared = call(share_kernel, f32(GROUPS * TILES_PER, 128), [], own, from_prev, from_next)
    everyone = exchange(shared)
    gradient = call(
        functools.partial(gradient_kernel, scale),
        f32(LEV, ROWS, COLS),
        [vmem((LEV, 32, COLS), jnp.float32), vmem((COLS, 128), jnp.float32), vmem((COLS, 128), jnp.float32),
         vmem((GROUPS, CHUNK), jnp.float32)],
        everyone, ens, before, after,
    )
    advected = moved[:, :LEV].transpose(1, 2, 0).reshape(LEV, 1, FINE_R * FINE_C)
    return (advected, gradient[None])


def solution(mesh):
    return jax.shard_map(
        shards,
        mesh=mesh,
        in_specs=(
            P("mem", None, "band", None),
            P("mem", None, "band", None),
            P("band"),
            P("band"),
            P(None, ("band", "mem"), None),
            P(("band", "mem"), None),
            P(None, ("band", "mem"), None),
            P(("band", "mem"), None),
        ),
        out_specs=(P(None, ("band", "mem"), None), P("mem", None, "band", None)),
        check_vma=False,
    )
```

```python
import functools
import math

import jax
import jax.numpy as jnp
from jax import lax
from jax.experimental import pallas as pl
from jax.experimental.pallas import tpu as pltpu
from jax.sharding import PartitionSpec as P

LEV = 12
LPAD = 16
ROWS = 16
COLS = 512
CHIPS = 32
BANDS = 8
BLOCK = 8
FRAME = BLOCK + 2
FINE_R = 48
FINE_C = 24
NOBS = 256
MAIN = LEV * ROWS
Q = MAIN + 2 * LEV
TILES = 17
CHUNK = TILES * 128

advect_rate = 0.25
highest = lax.Precision.HIGHEST


def lon_smooth(x):
    axis = x.ndim - 1
    return 0.25 * pltpu.roll(x, 1, axis) + 0.5 * x + 0.25 * pltpu.roll(x, COLS - 1, axis)


def interp(j):
    n = 2 * j + 4
    return n // 6, (n % 6) / 6.0


def halo_kernel(alpha_ref, ens_ref, last_ref, first_ref):
    last_ref[0] = alpha_ref[:, ROWS - 2, :]
    last_ref[1] = alpha_ref[:, ROWS - 1, :]
    last_ref[2] = ens_ref[:, ROWS - 1, :].astype(jnp.float32)
    first_ref[0] = alpha_ref[:, 0, :]
    first_ref[1] = alpha_ref[:, 1, :]
    first_ref[2] = ens_ref[:, 0, :].astype(jnp.float32)


def product_kernel(scale, core_ref, alpha_ref, ens_ref, prev_ref, next_ref, keep_ref, send_ref, pad, x_ref, xt_lo, xt_hi, flat):
    pad[:, 8:24, :] = alpha_ref[...]
    pad[:, 7, :] = prev_ref[1]
    pad[:, 24, :] = next_ref[0]
    body = 0.25 * pad[:, 7:23, :] + 0.5 * alpha_ref[...] + 0.25 * pad[:, 9:25, :]
    body = lon_smooth(body) * (ens_ref[...].astype(jnp.float32) * scale)
    top = 0.25 * prev_ref[0] + 0.5 * prev_ref[1] + 0.25 * alpha_ref[:, 0, :]
    low = 0.25 * alpha_ref[:, ROWS - 1, :] + 0.5 * next_ref[0] + 0.25 * next_ref[1]
    x_ref[:MAIN, :] = body.reshape(MAIN, COLS)
    x_ref[MAIN : MAIN + LEV, :] = lon_smooth(top) * (prev_ref[2] * scale)
    x_ref[MAIN + LEV : Q, :] = lon_smooth(low) * (next_ref[2] * scale)
    x_ref[Q:, :] = jnp.zeros((256 - Q, COLS), jnp.float32)
    for half, xt in enumerate((xt_lo, xt_hi)):
        xt[8 : 8 + COLS, :] = x_ref[128 * half : 128 * (half + 1), :].T
        xt[7:8, :] = xt[7 + COLS : 8 + COLS, :]
        xt[8 + COLS : 9 + COLS, :] = xt[8:9, :]
    flat[:, :, FRAME * Q :] = jnp.zeros((2, CHIPS, CHUNK - FRAME * Q), jnp.float32)
    for core in range(2):
        for c in range(FRAME):
            rows = pl.ds(7 + c + BLOCK * core, CHIPS, stride=2 * BLOCK)
            flat[core, :, c * Q : c * Q + 128] = xt_lo[rows, :]
            flat[core, :, c * Q + 128 : (c + 1) * Q] = xt_hi[rows, :][:, : Q - 128]
    first = core_ref[0] == 0
    for t in range(TILES):
        even = flat[0, :, 128 * t : 128 * (t + 1)]
        odd = flat[1, :, 128 * t : 128 * (t + 1)]
        keep_ref[pl.ds(t, CHIPS, stride=TILES), :] = jnp.where(first, even, odd)
        send_ref[pl.ds(t, CHIPS, stride=TILES), :] = jnp.where(first, odd, even)


def tile_kernel(band_ref, g_ref, bg_ref, lat_ref, obs_ref, adv_ref, own_ref, edge_ref, flat):
    for t in range(TILES):
        part = g_ref[pl.ds(t, CHIPS, stride=TILES), :]
        flat[0:1, 128 * t : 128 * (t + 1)] = jnp.sum(part, axis=0, keepdims=True)
    q = lax.broadcasted_iota(jnp.int32, (1, Q), 1)
    spot = jnp.where(q < MAIN, (q & 15) + 1, jnp.where(q < MAIN + LEV, 0, ROWS + 1))
    level = jnp.where(q < MAIN, q >> 4, jnp.where(q < MAIN + LEV, q - MAIN, q - MAIN - LEV))
    mask = lax.broadcasted_iota(jnp.int32, (LPAD, Q), 0) == level
    low = lat_ref[:, 0:1] + 1.0
    weight = lat_ref[:, 1:2]

    def table(place):
        place = place.astype(jnp.float32)
        return jnp.where(place == low, 1.0 - weight, 0.0) + jnp.where(place == low + 1.0, weight, 0.0)

    lat = table(spot)
    spread = [jnp.where(mask, flat[0:1, c * Q : (c + 1) * Q], 0.0) for c in range(FRAME)]
    lat_rows = lax.dot_general(jnp.concatenate(spread, axis=0), lat, (((1,), (1,)), ((), ())), precision=highest,
                               preferred_element_type=jnp.float32).reshape(FRAME, LPAD, FINE_R)
    state = []
    for j in range(-1, FINE_C + 1):
        lo, f = interp(j)
        state.append((1.0 - f) * lat_rows[lo] + f * lat_rows[lo + 1] + bg_ref[j + 1])
    slope = [0.5 * (state[j + 2] - state[j]) for j in range(FINE_C)]
    model = [state[j + 1] - advect_rate * state[j + 1] * slope[j] for j in range(FINE_C)]
    for j in range(FINE_C):
        adv_ref[j] = model[j]
    value = obs_ref[0:LPAD, :]
    precision = obs_ref[LPAD : LPAD + 1, :]
    row = obs_ref[LPAD + 1 : LPAD + 2, :]
    col = obs_ref[LPAD + 2 : LPAD + 3, :]
    fine_row = lax.broadcasted_iota(jnp.int32, (FINE_R, NOBS), 0).astype(jnp.float32)
    pick_row = jnp.where(fine_row == row, 1.0, 0.0)
    pick_col = [jnp.where(col == float(j), 1.0, 0.0) for j in range(FINE_C)]
    seen = jnp.dot(jnp.concatenate(model, axis=0), pick_row, precision=highest,
                   preferred_element_type=jnp.float32).reshape(FINE_C, LPAD, NOBS)
    observed = sum(pick_col[j] * seen[j] for j in range(FINE_C))
    weighted = precision * (observed - value)
    back = jnp.concatenate([pick_col[j] * weighted for j in range(FINE_C)], axis=0)
    cot = lax.dot_general(back, pick_row, (((1,), (1,)), ((), ())), precision=highest,
                          preferred_element_type=jnp.float32).reshape(FINE_C, LPAD, FINE_R)
    half_rate = 0.5 * advect_rate
    flux = [half_rate * state[j + 1] * cot[j] for j in range(FINE_C)]
    total = [None] * FRAME
    for j in range(-1, FINE_C + 1):
        adj = None
        if 0 <= j < FINE_C:
            adj = cot[j] - advect_rate * cot[j] * slope[j]
        if j + 1 < FINE_C:
            adj = flux[j + 1] if adj is None else adj + flux[j + 1]
        if j - 1 >= 0:
            adj = -flux[j - 1] if adj is None else adj - flux[j - 1]
        lo, f = interp(j)
        for c, w in ((lo, 1.0 - f), (lo + 1, f)):
            if w:
                total[c] = w * adj if total[c] is None else total[c] + w * adj
    coarse = jnp.concatenate(total, axis=0)

    def to_coarse(lat):
        wide = jnp.dot(coarse, lat, precision=highest, preferred_element_type=jnp.float32).reshape(FRAME, LPAD, Q)
        for c in range(FRAME):
            flat[0:1, c * Q : (c + 1) * Q] = jnp.sum(jnp.where(mask, wide[c], 0.0), axis=0, keepdims=True)

    band = band_ref[0]
    edge_ref[...] = jnp.zeros_like(edge_ref)
    for place, off, ok in ((spot + ROWS, 1, band < BANDS - 1), (spot - ROWS, -1, band > 0)):
        to_coarse(table(place))

        @pl.when(ok)
        def _():
            for t in range(TILES):
                edge_ref[pl.ds((band + off) * TILES + t, 1), :] = flat[0:1, 128 * t : 128 * (t + 1)]

    to_coarse(lat)
    for t in range(TILES):
        own_ref[t : t + 1, :] = flat[0:1, 128 * t : 128 * (t + 1)]


def share_kernel(own_ref, edge_ref, out_ref):
    total = own_ref[...]
    for b in range(BANDS):
        total = total + edge_ref[TILES * b : TILES * (b + 1), :]
    for m in range(CHIPS):
        out_ref[TILES * m : TILES * (m + 1), :] = total


def gradient_kernel(scale, g_ref, ens_ref, prev_ref, next_ref, out_ref, pad, xt_lo, xt_hi, flat):
    for core in range(2):
        for t in range(TILES):
            flat[core, :, 128 * t : 128 * (t + 1)] = g_ref[pl.ds(core * CHIPS * TILES + t, CHIPS, stride=TILES), :]
    slots = [[flat[core, :, c * Q : (c + 1) * Q] for c in range(FRAME)] for core in range(2)]
    even, odd = slots
    even_first = even[1] + pltpu.roll(odd[FRAME - 1], 1, 0)
    even_last = even[BLOCK] + odd[0]
    odd_first = odd[1] + even[FRAME - 1]
    odd_last = odd[BLOCK] + pltpu.roll(even[0], CHIPS - 1, 0)
    even[1], even[BLOCK], odd[1], odd[BLOCK] = even_first, even_last, odd_first, odd_last
    for core in range(2):
        for c in range(1, BLOCK + 1):
            rows = pl.ds(c - 1 + BLOCK * core, CHIPS, stride=2 * BLOCK)
            xt_lo[rows, :] = slots[core][c][:, :128]
            xt_hi[rows, : Q - 128] = slots[core][c][:, 128:]
    lo = xt_lo[...].T * scale
    hi = xt_hi[...].T * scale
    field = jnp.concatenate([lo, hi[: MAIN - 128, :]], axis=0).reshape(LEV, ROWS, COLS) * ens_ref[...].astype(jnp.float32)
    pad[:, 8:24, :] = field
    pad[:, 7, :] = hi[MAIN - 128 : MAIN - 128 + LEV, :] * prev_ref[2]
    pad[:, 24, :] = hi[MAIN - 128 + LEV : Q - 128, :] * next_ref[2]
    out_ref[...] = lon_smooth(0.25 * pad[:, 7:23, :] + 0.5 * field + 0.25 * pad[:, 9:25, :])


def call(kernel, out, scratch, *args):
    def spec(x):
        return pl.BlockSpec(memory_space=pltpu.SMEM if x.dtype == jnp.int32 else pltpu.VMEM)

    return pl.pallas_call(
        kernel,
        out_shape=out,
        in_specs=[spec(x) for x in args],
        out_specs=jax.tree.map(spec, out),
        scratch_shapes=[pltpu.VMEM(shape, jnp.float32) for shape in scratch],
        compiler_params=pltpu.CompilerParams(vmem_limit_bytes=40 * 1024 * 1024),
    )(*args)


def f32(*shape):
    return jax.ShapeDtypeStruct(shape, jnp.float32)


def both_ways(up_value, down_value, axis, size, wrap):
    up = [(i, (i + 1) % size) for i in range(size if wrap else size - 1)]
    down = [(j, i) for i, j in up]
    return lax.ppermute(up_value, axis, up), lax.ppermute(down_value, axis, down)


def exchange(flat, axis, size):
    parts = lax.all_to_all(flat.reshape(size, 1, CHUNK), axis, 0, 0, tiled=True)
    return parts.reshape(size * TILES, 128)


def shards(ensemble, alpha, lat_lower, lat_weight, background, obs_cell, obs_value, obs_precision):
    scale = 1.0 / math.sqrt(2 * CHIPS - 1)
    core = lax.axis_index("core").astype(jnp.int32).reshape(1)
    band = lax.axis_index("band").astype(jnp.int32).reshape(1)
    ens = ensemble[0]
    alf = alpha[0]
    last, first = call(halo_kernel, (f32(3, LEV, COLS), f32(3, LEV, COLS)), [], alf, ens)
    before, after = both_ways(last, first, "band", BANDS, False)

    grid = background.reshape(LEV, FINE_R, FINE_C).transpose(2, 0, 1)
    left, right = both_ways(grid[FINE_C - 1], grid[0], ("chip", "core"), 2 * CHIPS, True)
    obs = jnp.concatenate(
        [jnp.pad(obs_value[:, 0, :], ((0, LPAD - LEV), (0, 0))), obs_precision, (obs_cell // FINE_C).astype(jnp.float32),
         (obs_cell % FINE_C).astype(jnp.float32), jnp.zeros((24 - LPAD - 3, NOBS), jnp.float32)], axis=0)
    lat = jnp.stack([lat_lower.astype(jnp.float32), lat_weight], axis=1)
    wide = jnp.concatenate([left[None], grid, right[None]], axis=0)
    wide = jnp.pad(wide, ((0, 0), (0, LPAD - LEV), (0, 0)))
    before, after, wide, obs, lat = lax.optimization_barrier((before, after, wide, obs, lat))

    keep, send = call(
        functools.partial(product_kernel, scale),
        (f32(CHIPS * TILES, 128), f32(CHIPS * TILES, 128)),
        [(LEV, 32, COLS), (256, COLS), (COLS + 16, 128), (COLS + 16, 128), (2, CHIPS, CHUNK)],
        core, alf, ens, before, after,
    )
    pair = keep + lax.ppermute(send, "core", [(0, 1), (1, 0)])
    gathered = exchange(pair, "chip", CHIPS)
    moved, own, edge = call(
        tile_kernel,
        (f32(FINE_C, LPAD, FINE_R), f32(TILES, 128), f32(BANDS * TILES, 128)),
        [(8, CHUNK)],
        band, gathered, wide, lat, obs,
    )
    edge = exchange(edge, "band", BANDS)
    shared = call(share_kernel, f32(CHIPS * TILES, 128), [], own, edge)
    everyone = lax.all_gather(exchange(shared, "chip", CHIPS), "core", axis=0, tiled=True)
    gradient = call(
        functools.partial(gradient_kernel, scale),
        f32(LEV, ROWS, COLS),
        [(LEV, 32, COLS), (COLS, 128), (COLS, 128), (2, CHIPS, CHUNK)],
        everyone, ens, before, after,
    )
    advected = moved[:, :LEV].transpose(1, 2, 0).reshape(LEV, 1, FINE_R * FINE_C)
    return (advected, gradient[None])


def solution(mesh):
    member = ("chip", "core")
    tile = ("band", "chip", "core")
    return jax.shard_map(
        shards,
        mesh=jax.sharding.Mesh(mesh.devices.reshape(CHIPS, 2, BANDS), ("chip", "core", "band")),
        in_specs=(
            P(member, None, "band", None),
            P(member, None, "band", None),
            P("band"),
            P("band"),
            P(None, tile, None),
            P(tile, None),
            P(None, tile, None),
            P(tile, None),
        ),
        out_specs=(P(None, tile, None), P(member, None, "band", None)),
        check_vma=False,
    )
```

```python
import functools
import math

import jax
import jax.numpy as jnp
from jax import lax
from jax.experimental import pallas as pl
from jax.experimental.pallas import tpu as pltpu
from jax.sharding import PartitionSpec as P

LEV = 12
LPAD = 16
ROWS = 16
COLS = 512
CHIPS = 32
BANDS = 8
BLOCK = 8
FRAME = BLOCK + 2
FINE_R = 48
FINE_C = 24
NOBS = 256
MAIN = LEV * ROWS
Q = MAIN + 2 * LEV
TILES = 17
CHUNK = TILES * 128
SIDE = LEV * FINE_R
SIDE_T = 5
WIDE = TILES + SIDE_T

advect_rate = 0.25
highest = lax.Precision.HIGHEST


def lon_smooth(x):
    axis = x.ndim - 1
    return 0.25 * pltpu.roll(x, 1, axis) + 0.5 * x + 0.25 * pltpu.roll(x, COLS - 1, axis)


def interp(j):
    n = 2 * j + 4
    return n // 6, (n % 6) / 6.0


def halo_kernel(alpha_hbm, ens_hbm, last_ref, first_ref, alpha_ref, ens_ref, sems):
    copies = [pltpu.make_async_copy(alpha_hbm, alpha_ref, sems.at[0]), pltpu.make_async_copy(ens_hbm, ens_ref, sems.at[1])]
    for copy in copies:
        copy.start()
    for copy in copies:
        copy.wait()
    last_ref[0] = alpha_ref[:, ROWS - 2, :]
    last_ref[1] = alpha_ref[:, ROWS - 1, :]
    last_ref[2] = ens_ref[:, ROWS - 1, :].astype(jnp.float32)
    first_ref[0] = alpha_ref[:, 0, :]
    first_ref[1] = alpha_ref[:, 1, :]
    first_ref[2] = ens_ref[:, 0, :].astype(jnp.float32)


def product_kernel(scale, spot_ref, alpha_ref, ens_ref, prev_ref, next_ref, sides_ref, keep_ref, send_ref, pad, x_ref, xt_lo, xt_hi, flat):
    pad[:, 8:24, :] = alpha_ref[...]
    pad[:, 7, :] = prev_ref[1]
    pad[:, 24, :] = next_ref[0]
    body = 0.25 * pad[:, 7:23, :] + 0.5 * alpha_ref[...] + 0.25 * pad[:, 9:25, :]
    body = lon_smooth(body) * (ens_ref[...].astype(jnp.float32) * scale)
    top = 0.25 * prev_ref[0] + 0.5 * prev_ref[1] + 0.25 * alpha_ref[:, 0, :]
    low = 0.25 * alpha_ref[:, ROWS - 1, :] + 0.5 * next_ref[0] + 0.25 * next_ref[1]
    x_ref[:MAIN, :] = body.reshape(MAIN, COLS)
    x_ref[MAIN : MAIN + LEV, :] = lon_smooth(top) * (prev_ref[2] * scale)
    x_ref[MAIN + LEV : Q, :] = lon_smooth(low) * (next_ref[2] * scale)
    x_ref[Q:, :] = jnp.zeros((256 - Q, COLS), jnp.float32)
    for half, xt in enumerate((xt_lo, xt_hi)):
        xt[8 : 8 + COLS, :] = x_ref[128 * half : 128 * (half + 1), :].T
        xt[7:8, :] = xt[7 + COLS : 8 + COLS, :]
        xt[8 + COLS : 9 + COLS, :] = xt[8:9, :]
    flat[:, :, FRAME * Q :] = jnp.zeros((2, CHIPS, CHUNK - FRAME * Q), jnp.float32)
    for core in range(2):
        for c in range(FRAME):
            rows = pl.ds(7 + c + BLOCK * core, CHIPS, stride=2 * BLOCK)
            flat[core, :, c * Q : c * Q + 128] = xt_lo[rows, :]
            flat[core, :, c * Q + 128 : (c + 1) * Q] = xt_hi[rows, :][:, : Q - 128]
    first = spot_ref[0] == 0
    for t in range(TILES):
        even = flat[0, :, 128 * t : 128 * (t + 1)]
        odd = flat[1, :, 128 * t : 128 * (t + 1)]
        keep_ref[pl.ds(t, CHIPS, stride=WIDE), :] = jnp.where(first, even, odd)
        send_ref[pl.ds(t, CHIPS, stride=WIDE), :] = jnp.where(first, odd, even)
    chip = spot_ref[1]
    other = lax.rem(chip + jnp.where(first, CHIPS - 1, 1), CHIPS)
    target = lax.broadcasted_iota(jnp.int32, (CHIPS, 128), 0)
    for t in range(SIDE_T):
        lanes = slice(128 * t, 128 * (t + 1))
        left, right = sides_ref[0:1, lanes], sides_ref[1:2, lanes]
        near = jnp.where(first, right, left)
        far = jnp.where(first, left, right)
        side = jnp.where(target == chip, near, jnp.where(target == other, far, 0.0))
        keep_ref[pl.ds(TILES + t, CHIPS, stride=WIDE), :] = jnp.zeros((CHIPS, 128), jnp.float32)
        send_ref[pl.ds(TILES + t, CHIPS, stride=WIDE), :] = side


def tile_kernel(spot_ref, g_ref, bg_ref, lat_ref, obs_ref, adv_ref, own_ref, up_ref, down_ref, flat, sides):
    for t in range(TILES):
        part = g_ref[pl.ds(t, CHIPS, stride=WIDE), :]
        flat[0:1, 128 * t : 128 * (t + 1)] = jnp.sum(part, axis=0, keepdims=True)
    first = spot_ref[0] == 0
    chip = spot_ref[1]
    other = lax.rem(chip + jnp.where(first, CHIPS - 1, 1), CHIPS)
    for s, source in enumerate((chip, other)):
        for t in range(SIDE_T):
            sides[s : s + 1, 128 * t : 128 * (t + 1)] = g_ref[pl.ds(source * WIDE + TILES + t, 1), :]
    none = jnp.zeros((1, FINE_R), jnp.float32)
    near, far = (jnp.concatenate([sides[s : s + 1, FINE_R * l : FINE_R * (l + 1)] for l in range(LEV)] + [none] * (LPAD - LEV), axis=0)
                 for s in range(2))
    ground = [jnp.where(first, far, near)] + [bg_ref[j] for j in range(FINE_C)] + [jnp.where(first, near, far)]
    q = lax.broadcasted_iota(jnp.int32, (1, Q), 1)
    spot = jnp.where(q < MAIN, (q & 15) + 1, jnp.where(q < MAIN + LEV, 0, ROWS + 1))
    level = jnp.where(q < MAIN, q >> 4, jnp.where(q < MAIN + LEV, q - MAIN, q - MAIN - LEV))
    mask = lax.broadcasted_iota(jnp.int32, (LPAD, Q), 0) == level
    low = lat_ref[:, 0:1] + 1.0
    weight = lat_ref[:, 1:2]

    def table(place):
        place = place.astype(jnp.float32)
        return jnp.where(place == low, 1.0 - weight, 0.0) + jnp.where(place == low + 1.0, weight, 0.0)

    lat = table(spot)
    spread = [jnp.where(mask, flat[0:1, c * Q : (c + 1) * Q], 0.0) for c in range(FRAME)]
    lat_rows = lax.dot_general(jnp.concatenate(spread, axis=0), lat, (((1,), (1,)), ((), ())), precision=highest,
                               preferred_element_type=jnp.float32).reshape(FRAME, LPAD, FINE_R)
    state = []
    for j in range(-1, FINE_C + 1):
        lo, f = interp(j)
        state.append((1.0 - f) * lat_rows[lo] + f * lat_rows[lo + 1] + ground[j + 1])
    slope = [0.5 * (state[j + 2] - state[j]) for j in range(FINE_C)]
    model = [state[j + 1] - advect_rate * state[j + 1] * slope[j] for j in range(FINE_C)]
    for j in range(FINE_C):
        adv_ref[j] = model[j]
    value = obs_ref[0:LPAD, :]
    precision = obs_ref[LPAD : LPAD + 1, :]
    row = obs_ref[LPAD + 1 : LPAD + 2, :]
    col = obs_ref[LPAD + 2 : LPAD + 3, :]
    fine_row = lax.broadcasted_iota(jnp.int32, (FINE_R, NOBS), 0).astype(jnp.float32)
    pick_row = jnp.where(fine_row == row, 1.0, 0.0)
    pick_col = [jnp.where(col == float(j), 1.0, 0.0) for j in range(FINE_C)]
    seen = jnp.dot(jnp.concatenate(model, axis=0), pick_row, precision=highest,
                   preferred_element_type=jnp.float32).reshape(FINE_C, LPAD, NOBS)
    observed = sum(pick_col[j] * seen[j] for j in range(FINE_C))
    weighted = precision * (observed - value)
    back = jnp.concatenate([pick_col[j] * weighted for j in range(FINE_C)], axis=0)
    cot = lax.dot_general(back, pick_row, (((1,), (1,)), ((), ())), precision=highest,
                          preferred_element_type=jnp.float32).reshape(FINE_C, LPAD, FINE_R)
    half_rate = 0.5 * advect_rate
    flux = [half_rate * state[j + 1] * cot[j] for j in range(FINE_C)]
    total = [None] * FRAME
    for j in range(-1, FINE_C + 1):
        adj = None
        if 0 <= j < FINE_C:
            adj = cot[j] - advect_rate * cot[j] * slope[j]
        if j + 1 < FINE_C:
            adj = flux[j + 1] if adj is None else adj + flux[j + 1]
        if j - 1 >= 0:
            adj = -flux[j - 1] if adj is None else adj - flux[j - 1]
        lo, f = interp(j)
        for c, w in ((lo, 1.0 - f), (lo + 1, f)):
            if w:
                total[c] = w * adj if total[c] is None else total[c] + w * adj
    coarse = jnp.concatenate(total, axis=0)

    def to_coarse(lat, ref):
        wide = jnp.dot(coarse, lat, precision=highest, preferred_element_type=jnp.float32).reshape(FRAME, LPAD, Q)
        for c in range(FRAME):
            flat[0:1, c * Q : (c + 1) * Q] = jnp.sum(jnp.where(mask, wide[c], 0.0), axis=0, keepdims=True)
        for t in range(TILES):
            ref[t : t + 1, :] = flat[0:1, 128 * t : 128 * (t + 1)]

    to_coarse(lat, own_ref)
    to_coarse(table(spot + ROWS), up_ref)
    to_coarse(table(spot - ROWS), down_ref)


def share_kernel(own_ref, prev_ref, next_ref, out_ref):
    total = own_ref[...] + prev_ref[...] + next_ref[...]
    for m in range(CHIPS):
        out_ref[TILES * m : TILES * (m + 1), :] = total


def gradient_kernel(scale, g_ref, ens_ref, prev_ref, next_ref, out_ref, pad, xt_lo, xt_hi, flat):
    for core in range(2):
        for t in range(TILES):
            flat[core, :, 128 * t : 128 * (t + 1)] = g_ref[pl.ds(core * CHIPS * TILES + t, CHIPS, stride=TILES), :]
    slots = [[flat[core, :, c * Q : (c + 1) * Q] for c in range(FRAME)] for core in range(2)]
    even, odd = slots
    even_first = even[1] + pltpu.roll(odd[FRAME - 1], 1, 0)
    even_last = even[BLOCK] + odd[0]
    odd_first = odd[1] + even[FRAME - 1]
    odd_last = odd[BLOCK] + pltpu.roll(even[0], CHIPS - 1, 0)
    even[1], even[BLOCK], odd[1], odd[BLOCK] = even_first, even_last, odd_first, odd_last
    for core in range(2):
        for c in range(1, BLOCK + 1):
            rows = pl.ds(c - 1 + BLOCK * core, CHIPS, stride=2 * BLOCK)
            xt_lo[rows, :] = slots[core][c][:, :128]
            xt_hi[rows, : Q - 128] = slots[core][c][:, 128:]
    lo = xt_lo[...].T * scale
    hi = xt_hi[...].T * scale
    field = jnp.concatenate([lo, hi[: MAIN - 128, :]], axis=0).reshape(LEV, ROWS, COLS) * ens_ref[...].astype(jnp.float32)
    pad[:, 8:24, :] = field
    pad[:, 7, :] = hi[MAIN - 128 : MAIN - 128 + LEV, :] * prev_ref[2]
    pad[:, 24, :] = hi[MAIN - 128 + LEV : Q - 128, :] * next_ref[2]
    out_ref[...] = lon_smooth(0.25 * pad[:, 7:23, :] + 0.5 * field + 0.25 * pad[:, 9:25, :])


def call(kernel, out, scratch, *args, hbm=False, sems=()):
    def spec(x):
        return pl.BlockSpec(memory_space=pltpu.SMEM if x.dtype == jnp.int32 else pltpu.VMEM)

    return pl.pallas_call(
        kernel,
        out_shape=out,
        in_specs=[pl.BlockSpec(memory_space=pltpu.HBM) if hbm else spec(x) for x in args],
        out_specs=jax.tree.map(spec, out),
        scratch_shapes=[pltpu.VMEM(shape, jnp.float32) for shape in scratch] + list(sems),
        compiler_params=pltpu.CompilerParams(vmem_limit_bytes=40 * 1024 * 1024),
    )(*args)


def f32(*shape):
    return jax.ShapeDtypeStruct(shape, jnp.float32)


def both_ways(up_value, down_value, axis, size, wrap):
    up = [(i, (i + 1) % size) for i in range(size if wrap else size - 1)]
    down = [(j, i) for i, j in up]
    return lax.ppermute(up_value, axis, up), lax.ppermute(down_value, axis, down)


def exchange(flat, tiles):
    parts = lax.all_to_all(flat.reshape(CHIPS, 1, tiles * 128), "chip", 0, 0, tiled=True)
    return parts.reshape(CHIPS * tiles, 128)


def shards(ensemble, alpha, lat_lower, lat_weight, background, obs_cell, obs_value, obs_precision):
    scale = 1.0 / math.sqrt(2 * CHIPS - 1)
    spot = jnp.stack([lax.axis_index("core"), lax.axis_index("chip")]).astype(jnp.int32)
    last, first, alf, ens = call(
        halo_kernel,
        (f32(3, LEV, COLS), f32(3, LEV, COLS), f32(LEV, ROWS, COLS), jax.ShapeDtypeStruct((LEV, ROWS, COLS), jnp.bfloat16)),
        [], alpha[0], ensemble[0], hbm=True, sems=[pltpu.SemaphoreType.DMA((2,))],
    )
    before, after = both_ways(last, first, "band", BANDS, False)

    grid = background.reshape(LEV, FINE_R, FINE_C).transpose(2, 0, 1)
    sides = jnp.stack([grid[0].reshape(SIDE), grid[FINE_C - 1].reshape(SIDE)])
    sides = jnp.pad(sides, ((0, 0), (0, SIDE_T * 128 - SIDE)))
    ground = jnp.pad(grid, ((0, 0), (0, LPAD - LEV), (0, 0)))
    obs = jnp.concatenate(
        [jnp.pad(obs_value[:, 0, :], ((0, LPAD - LEV), (0, 0))), obs_precision, (obs_cell // FINE_C).astype(jnp.float32),
         (obs_cell % FINE_C).astype(jnp.float32), jnp.zeros((24 - LPAD - 3, NOBS), jnp.float32)], axis=0)
    lat = jnp.stack([lat_lower.astype(jnp.float32), lat_weight], axis=1)
    before, after, ground, sides, obs, lat = lax.optimization_barrier((before, after, ground, sides, obs, lat))

    keep, send = call(
        functools.partial(product_kernel, scale),
        (f32(CHIPS * WIDE, 128), f32(CHIPS * WIDE, 128)),
        [(LEV, 32, COLS), (256, COLS), (COLS + 16, 128), (COLS + 16, 128), (2, CHIPS, CHUNK)],
        spot, alf, ens, before, after, sides,
    )
    pair = keep + lax.ppermute(send, "core", [(0, 1), (1, 0)])
    gathered = exchange(pair, WIDE)
    moved, own, up, down = call(
        tile_kernel,
        (f32(FINE_C, LPAD, FINE_R), f32(TILES, 128), f32(TILES, 128), f32(TILES, 128)),
        [(8, CHUNK), (8, SIDE_T * 128)],
        spot, gathered, ground, lat, obs,
    )
    from_prev, from_next = both_ways(up, down, "band", BANDS, False)
    shared = call(share_kernel, f32(CHIPS * TILES, 128), [], own, from_prev, from_next)
    everyone = lax.all_gather(exchange(shared, TILES), "core", axis=0, tiled=True)
    gradient = call(
        functools.partial(gradient_kernel, scale),
        f32(LEV, ROWS, COLS),
        [(LEV, 32, COLS), (COLS, 128), (COLS, 128), (2, CHIPS, CHUNK)],
        everyone, ens, before, after,
    )
    advected = moved[:, :LEV].transpose(1, 2, 0).reshape(LEV, 1, FINE_R * FINE_C)
    return (advected, gradient[None])


def solution(mesh):
    member = ("chip", "core")
    tile = ("band", "chip", "core")
    return jax.shard_map(
        shards,
        mesh=jax.sharding.Mesh(mesh.devices.reshape(CHIPS, 2, BANDS), ("chip", "core", "band")),
        in_specs=(
            P(member, None, "band", None),
            P(member, None, "band", None),
            P("band"),
            P("band"),
            P(None, tile, None),
            P(tile, None),
            P(None, tile, None),
            P(tile, None),
        ),
        out_specs=(P(None, tile, None), P(member, None, "band", None)),
        check_vma=False,
    )
```

```python
import functools
import math

import jax
import jax.numpy as jnp
from jax import lax
from jax.experimental import pallas as pl
from jax.experimental.pallas import tpu as pltpu
from jax.sharding import PartitionSpec as P

LEV = 12
LPAD = 16
ROWS = 16
COLS = 512
CHIPS = 32
BANDS = 8
BLOCK = 8
FRAME = BLOCK + 2
FINE_R = 48
FINE_C = 24
NOBS = 256
MAIN = LEV * ROWS
Q = MAIN + 2 * LEV
TILES = 17
CHUNK = TILES * 128
PAIR = CHIPS * TILES

advect_rate = 0.25
highest = lax.Precision.HIGHEST


def lon_smooth(x):
    axis = x.ndim - 1
    return 0.25 * pltpu.roll(x, 1, axis) + 0.5 * x + 0.25 * pltpu.roll(x, COLS - 1, axis)


def interp(j):
    n = 2 * j + 4
    return n // 6, (n % 6) / 6.0


def halo_kernel(alpha_hbm, ens_hbm, last_ref, first_ref, alpha_ref, ens_ref, sems):
    copies = [pltpu.make_async_copy(alpha_hbm, alpha_ref, sems.at[0]), pltpu.make_async_copy(ens_hbm, ens_ref, sems.at[1])]
    for copy in copies:
        copy.start()
    for copy in copies:
        copy.wait()
    last_ref[0] = alpha_ref[:, ROWS - 2, :]
    last_ref[1] = alpha_ref[:, ROWS - 1, :]
    last_ref[2] = ens_ref[:, ROWS - 1, :].astype(jnp.float32)
    first_ref[0] = alpha_ref[:, 0, :]
    first_ref[1] = alpha_ref[:, 1, :]
    first_ref[2] = ens_ref[:, 0, :].astype(jnp.float32)


def product_kernel(scale, spot_ref, alpha_ref, ens_ref, prev_ref, next_ref, sides_ref, keep_ref, send_ref, pad, x_ref, xt_lo, xt_hi, flat):
    pad[:, 8:24, :] = alpha_ref[...]
    pad[:, 7, :] = prev_ref[1]
    pad[:, 24, :] = next_ref[0]
    body = 0.25 * pad[:, 7:23, :] + 0.5 * alpha_ref[...] + 0.25 * pad[:, 9:25, :]
    body = lon_smooth(body) * (ens_ref[...].astype(jnp.float32) * scale)
    top = 0.25 * prev_ref[0] + 0.5 * prev_ref[1] + 0.25 * alpha_ref[:, 0, :]
    low = 0.25 * alpha_ref[:, ROWS - 1, :] + 0.5 * next_ref[0] + 0.25 * next_ref[1]
    x_ref[:MAIN, :] = body.reshape(MAIN, COLS)
    x_ref[MAIN : MAIN + LEV, :] = lon_smooth(top) * (prev_ref[2] * scale)
    x_ref[MAIN + LEV : Q, :] = lon_smooth(low) * (next_ref[2] * scale)
    x_ref[Q:, :] = jnp.zeros((256 - Q, COLS), jnp.float32)
    for half, xt in enumerate((xt_lo, xt_hi)):
        xt[8 : 8 + COLS, :] = x_ref[128 * half : 128 * (half + 1), :].T
        xt[7:8, :] = xt[7 + COLS : 8 + COLS, :]
        xt[8 + COLS : 9 + COLS, :] = xt[8:9, :]
    flat[:, :, FRAME * Q :] = jnp.zeros((2, CHIPS, CHUNK - FRAME * Q), jnp.float32)
    for core in range(2):
        for c in range(FRAME):
            rows = pl.ds(7 + c + BLOCK * core, CHIPS, stride=2 * BLOCK)
            flat[core, :, c * Q : c * Q + 128] = xt_lo[rows, :]
            flat[core, :, c * Q + 128 : (c + 1) * Q] = xt_hi[rows, :][:, : Q - 128]
    first = spot_ref[0] == 0
    for t in range(TILES):
        even = flat[0, :, 128 * t : 128 * (t + 1)]
        odd = flat[1, :, 128 * t : 128 * (t + 1)]
        keep_ref[pl.ds(t, CHIPS, stride=TILES), :] = jnp.where(first, even, odd)
        send_ref[pl.ds(t, CHIPS, stride=TILES), :] = jnp.where(first, odd, even)
    send_ref[PAIR:, :] = sides_ref[...]


def pair_kernel(keep_ref, got_ref, out_ref):
    out_ref[...] = keep_ref[...] + got_ref[:PAIR, :]


def split_dot(x, pick, dim):
    total = None
    for _ in range(3):
        part = x.astype(jnp.bfloat16)
        x = x - part.astype(jnp.float32)
        got = lax.dot_general(part, pick, (((1,), (dim,)), ((), ())), preferred_element_type=jnp.float32)
        total = got if total is None else total + got
    return total


def tile_kernel(spot_ref, g_ref, near_ref, far_ref, bg_ref, lat_ref, obs_ref, adv_ref, own_ref, edge_ref, flat):
    for t in range(TILES):
        part = g_ref[pl.ds(t, CHIPS, stride=TILES), :]
        flat[0:1, 128 * t : 128 * (t + 1)] = jnp.sum(part, axis=0, keepdims=True)
    first = spot_ref[0] == 0
    near, far = near_ref[...], far_ref[...]
    ground = [jnp.where(first, far, near)] + [bg_ref[j] for j in range(FINE_C)] + [jnp.where(first, near, far)]
    q = lax.broadcasted_iota(jnp.int32, (1, Q), 1)
    spot = jnp.where(q < MAIN, (q & 15) + 1, jnp.where(q < MAIN + LEV, 0, ROWS + 1))
    level = jnp.where(q < MAIN, q >> 4, jnp.where(q < MAIN + LEV, q - MAIN, q - MAIN - LEV))
    mask = lax.broadcasted_iota(jnp.int32, (LPAD, Q), 0) == level
    low = lat_ref[:, 0:1] + 1.0
    weight = lat_ref[:, 1:2]

    def table(place):
        place = place.astype(jnp.float32)
        return jnp.where(place == low, 1.0 - weight, 0.0) + jnp.where(place == low + 1.0, weight, 0.0)

    lat = table(spot)
    spread = [jnp.where(mask, flat[0:1, c * Q : (c + 1) * Q], 0.0) for c in range(FRAME)]
    lat_rows = lax.dot_general(jnp.concatenate(spread, axis=0), lat, (((1,), (1,)), ((), ())), precision=highest,
                               preferred_element_type=jnp.float32).reshape(FRAME, LPAD, FINE_R)
    state = []
    for j in range(-1, FINE_C + 1):
        lo, f = interp(j)
        state.append((1.0 - f) * lat_rows[lo] + f * lat_rows[lo + 1] + ground[j + 1])
    slope = [0.5 * (state[j + 2] - state[j]) for j in range(FINE_C)]
    model = [state[j + 1] - advect_rate * state[j + 1] * slope[j] for j in range(FINE_C)]
    for j in range(FINE_C):
        adv_ref[j] = model[j]
    value = obs_ref[0:LPAD, :]
    precision = obs_ref[LPAD : LPAD + 1, :]
    row = obs_ref[LPAD + 1 : LPAD + 2, :]
    col = obs_ref[LPAD + 2 : LPAD + 3, :]
    fine_row = lax.broadcasted_iota(jnp.int32, (FINE_R, NOBS), 0).astype(jnp.float32)
    pick_row = jnp.where(fine_row == row, 1.0, 0.0).astype(jnp.bfloat16)
    pick_col = [jnp.where(col == float(j), 1.0, 0.0) for j in range(FINE_C)]
    seen = split_dot(jnp.concatenate(model, axis=0), pick_row, 0).reshape(FINE_C, LPAD, NOBS)
    observed = sum(pick_col[j] * seen[j] for j in range(FINE_C))
    weighted = precision * (observed - value)
    back = jnp.concatenate([pick_col[j] * weighted for j in range(FINE_C)], axis=0)
    cot = split_dot(back, pick_row, 1).reshape(FINE_C, LPAD, FINE_R)
    half_rate = 0.5 * advect_rate
    flux = [half_rate * state[j + 1] * cot[j] for j in range(FINE_C)]
    total = [None] * FRAME
    for j in range(-1, FINE_C + 1):
        adj = None
        if 0 <= j < FINE_C:
            adj = cot[j] - advect_rate * cot[j] * slope[j]
        if j + 1 < FINE_C:
            adj = flux[j + 1] if adj is None else adj + flux[j + 1]
        if j - 1 >= 0:
            adj = -flux[j - 1] if adj is None else adj - flux[j - 1]
        lo, f = interp(j)
        for c, w in ((lo, 1.0 - f), (lo + 1, f)):
            if w:
                total[c] = w * adj if total[c] is None else total[c] + w * adj
    coarse = jnp.concatenate(total, axis=0)

    def to_coarse(lat, ref):
        wide = jnp.dot(coarse, lat, precision=highest, preferred_element_type=jnp.float32).reshape(FRAME, LPAD, Q)
        for c in range(FRAME):
            flat[0:1, c * Q : (c + 1) * Q] = jnp.sum(jnp.where(mask, wide[c], 0.0), axis=0, keepdims=True)
        for t in range(TILES):
            ref[t : t + 1, :] = flat[0:1, 128 * t : 128 * (t + 1)]

    to_coarse(lat, own_ref)
    to_coarse(table(jnp.where(spot < 2, spot + ROWS, spot - ROWS)), edge_ref)


def share_kernel(own_ref, prev_ref, next_ref, out_ref):
    shape = (TILES, 128)
    q = lax.rem(lax.broadcasted_iota(jnp.int32, shape, 0) * 128 + lax.broadcasted_iota(jnp.int32, shape, 1), Q)
    row = q & 15
    inner = q < MAIN
    from_prev = (inner & (row == 0)) | ((q >= MAIN) & (q < MAIN + LEV))
    from_next = (inner & (row == ROWS - 1)) | (q >= MAIN + LEV)
    total = own_ref[...] + jnp.where(from_prev, prev_ref[...], 0.0) + jnp.where(from_next, next_ref[...], 0.0)
    for m in range(CHIPS):
        out_ref[TILES * m : TILES * (m + 1), :] = total


def gradient_kernel(scale, g_ref, ens_ref, prev_ref, next_ref, out_ref, pad, xt_lo, xt_hi, flat):
    for core in range(2):
        for t in range(TILES):
            flat[core, :, 128 * t : 128 * (t + 1)] = g_ref[pl.ds(core * CHIPS * TILES + t, CHIPS, stride=TILES), :]
    slots = [[flat[core, :, c * Q : (c + 1) * Q] for c in range(FRAME)] for core in range(2)]
    even, odd = slots
    even_first = even[1] + pltpu.roll(odd[FRAME - 1], 1, 0)
    even_last = even[BLOCK] + odd[0]
    odd_first = odd[1] + even[FRAME - 1]
    odd_last = odd[BLOCK] + pltpu.roll(even[0], CHIPS - 1, 0)
    even[1], even[BLOCK], odd[1], odd[BLOCK] = even_first, even_last, odd_first, odd_last
    for core in range(2):
        for c in range(1, BLOCK + 1):
            rows = pl.ds(c - 1 + BLOCK * core, CHIPS, stride=2 * BLOCK)
            xt_lo[rows, :] = slots[core][c][:, :128]
            xt_hi[rows, : Q - 128] = slots[core][c][:, 128:]
    lo = xt_lo[...].T * scale
    hi = xt_hi[...].T * scale
    field = jnp.concatenate([lo, hi[: MAIN - 128, :]], axis=0).reshape(LEV, ROWS, COLS) * ens_ref[...].astype(jnp.float32)
    pad[:, 8:24, :] = field
    pad[:, 7, :] = hi[MAIN - 128 : MAIN - 128 + LEV, :] * prev_ref[2]
    pad[:, 24, :] = hi[MAIN - 128 + LEV : Q - 128, :] * next_ref[2]
    out_ref[...] = lon_smooth(0.25 * pad[:, 7:23, :] + 0.5 * field + 0.25 * pad[:, 9:25, :])


def call(kernel, out, scratch, *args, hbm=False, sems=()):
    def spec(x):
        return pl.BlockSpec(memory_space=pltpu.SMEM if x.dtype == jnp.int32 else pltpu.VMEM)

    return pl.pallas_call(
        kernel,
        out_shape=out,
        in_specs=[pl.BlockSpec(memory_space=pltpu.HBM) if hbm else spec(x) for x in args],
        out_specs=jax.tree.map(spec, out),
        scratch_shapes=[pltpu.VMEM(shape, jnp.float32) for shape in scratch] + list(sems),
        compiler_params=pltpu.CompilerParams(vmem_limit_bytes=40 * 1024 * 1024),
    )(*args)


def f32(*shape):
    return jax.ShapeDtypeStruct(shape, jnp.float32)


def both_ways(up_value, down_value, axis, size, wrap):
    up = [(i, (i + 1) % size) for i in range(size if wrap else size - 1)]
    down = [(j, i) for i, j in up]
    return lax.ppermute(up_value, axis, up), lax.ppermute(down_value, axis, down)


def exchange(flat, tiles):
    parts = lax.all_to_all(flat.reshape(CHIPS, 1, tiles * 128), "chip", 0, 0, tiled=True)
    return parts.reshape(CHIPS * tiles, 128)


def shards(ensemble, alpha, lat_lower, lat_weight, background, obs_cell, obs_value, obs_precision):
    scale = 1.0 / math.sqrt(2 * CHIPS - 1)
    spot = jnp.stack([lax.axis_index("core"), lax.axis_index("chip")]).astype(jnp.int32)
    last, first, alf, ens = call(
        halo_kernel,
        (f32(3, LEV, COLS), f32(3, LEV, COLS), f32(LEV, ROWS, COLS), jax.ShapeDtypeStruct((LEV, ROWS, COLS), jnp.bfloat16)),
        [], pltpu.with_memory_space_constraint(alpha[0], pltpu.HBM), pltpu.with_memory_space_constraint(ensemble[0], pltpu.HBM), hbm=True, sems=[pltpu.SemaphoreType.DMA((2,))],
    )
    before, after = both_ways(last, first, "band", BANDS, False)

    grid = background.reshape(LEV, FINE_R, FINE_C).transpose(2, 0, 1)
    first_core = lax.axis_index("core") == 0
    sides = jnp.where(first_core, grid[FINE_C - 1], grid[0])
    sides = jnp.pad(sides, ((0, LPAD - LEV), (0, 128 - FINE_R)))
    far = jnp.where(first_core, grid[0], grid[FINE_C - 1])
    size = 2 * CHIPS
    far = lax.ppermute(far, ("chip", "core"), [(i, (i + (1 if i % 2 else size - 1)) % size) for i in range(size)])
    far = jnp.pad(far, ((0, LPAD - LEV), (0, 0)))
    ground = jnp.pad(grid, ((0, 0), (0, LPAD - LEV), (0, 0)))
    obs = jnp.concatenate(
        [jnp.pad(obs_value[:, 0, :], ((0, LPAD - LEV), (0, 0))), obs_precision, (obs_cell // FINE_C).astype(jnp.float32),
         (obs_cell % FINE_C).astype(jnp.float32), jnp.zeros((24 - LPAD - 3, NOBS), jnp.float32)], axis=0)
    lat = jnp.stack([lat_lower.astype(jnp.float32), lat_weight], axis=1)
    before, after, ground, sides, obs, lat = lax.optimization_barrier((before, after, ground, sides, obs, lat))

    keep, send = call(
        functools.partial(product_kernel, scale),
        (f32(PAIR, 128), f32(PAIR + LPAD, 128)),
        [(LEV, 32, COLS), (256, COLS), (COLS + 16, 128), (COLS + 16, 128), (2, CHIPS, CHUNK)],
        spot, alf, ens, before, after, sides,
    )
    got = lax.ppermute(send, "core", [(0, 1), (1, 0)])
    gathered = exchange(call(pair_kernel, f32(PAIR, 128), [], keep, got), TILES)
    moved, own, edge = call(
        tile_kernel,
        (f32(FINE_C, LPAD, FINE_R), f32(TILES, 128), f32(TILES, 128)),
        [(8, CHUNK)],
        spot, gathered, got[PAIR:, :FINE_R], far, ground, lat, obs,
    )
    from_prev, from_next = both_ways(edge, edge, "band", BANDS, False)
    shared = call(share_kernel, f32(CHIPS * TILES, 128), [], own, from_prev, from_next)
    everyone = lax.all_gather(exchange(shared, TILES), "core", axis=0, tiled=True)
    gradient = call(
        functools.partial(gradient_kernel, scale),
        f32(LEV, ROWS, COLS),
        [(LEV, 32, COLS), (COLS, 128), (COLS, 128), (2, CHIPS, CHUNK)],
        everyone, ens, before, after,
    )
    advected = moved[:, :LEV].transpose(1, 2, 0).reshape(LEV, 1, FINE_R * FINE_C)
    return (advected, gradient[None])


def solution(mesh):
    member = ("chip", "core")
    tile = ("band", "chip", "core")
    return jax.shard_map(
        shards,
        mesh=jax.sharding.Mesh(mesh.devices.reshape(CHIPS, 2, BANDS), ("chip", "core", "band")),
        in_specs=(
            P(member, None, "band", None),
            P(member, None, "band", None),
            P("band"),
            P("band"),
            P(None, tile, None),
            P(tile, None),
            P(None, tile, None),
            P(tile, None),
        ),
        out_specs=(P(None, tile, None), P(member, None, "band", None)),
        check_vma=False,
    )
```

```python
import functools
import math

import jax
import jax.numpy as jnp
from jax import lax
from jax.experimental import pallas as pl
from jax.experimental.pallas import tpu as pltpu
from jax.sharding import PartitionSpec as P

LEV = 12
LPAD = 16
ROWS = 16
COLS = 512
CHIPS = 32
BANDS = 8
BLOCK = 8
FRAME = BLOCK + 2
FINE_R = 48
FINE_C = 24
NOBS = 256
MAIN = LEV * ROWS
Q = MAIN + 2 * LEV
TILES = 17
CHUNK = TILES * 128
PAIR = CHIPS * TILES

advect_rate = 0.25
highest = lax.Precision.HIGHEST


def lon_smooth(x):
    axis = x.ndim - 1
    return 0.25 * pltpu.roll(x, 1, axis) + 0.5 * x + 0.25 * pltpu.roll(x, COLS - 1, axis)


def interp(j):
    n = 2 * j + 4
    return n // 6, (n % 6) / 6.0


def halo_kernel(alpha_hbm, ens_hbm, last_ref, first_ref, alpha_ref, ens_ref, sems):
    copies = [pltpu.make_async_copy(alpha_hbm, alpha_ref, sems.at[0]), pltpu.make_async_copy(ens_hbm, ens_ref, sems.at[1])]
    for copy in copies:
        copy.start()
    for copy in copies:
        copy.wait()
    last_ref[0] = alpha_ref[:, ROWS - 2, :]
    last_ref[1] = alpha_ref[:, ROWS - 1, :]
    last_ref[2] = ens_ref[:, ROWS - 1, :].astype(jnp.float32)
    first_ref[0] = alpha_ref[:, 0, :]
    first_ref[1] = alpha_ref[:, 1, :]
    first_ref[2] = ens_ref[:, 0, :].astype(jnp.float32)


def product_kernel(scale, spot_ref, alpha_ref, ens_ref, prev_ref, next_ref, sides_ref, keep_ref, send_ref, pad, x_ref, xt_lo, xt_hi, flat):
    pad[:, 8:24, :] = alpha_ref[...]
    pad[:, 7, :] = prev_ref[1]
    pad[:, 24, :] = next_ref[0]
    body = 0.25 * pad[:, 7:23, :] + 0.5 * alpha_ref[...] + 0.25 * pad[:, 9:25, :]
    body = lon_smooth(body) * (ens_ref[...].astype(jnp.float32) * scale)
    top = 0.25 * prev_ref[0] + 0.5 * prev_ref[1] + 0.25 * alpha_ref[:, 0, :]
    low = 0.25 * alpha_ref[:, ROWS - 1, :] + 0.5 * next_ref[0] + 0.25 * next_ref[1]
    x_ref[:MAIN, :] = body.reshape(MAIN, COLS)
    x_ref[MAIN : MAIN + LEV, :] = lon_smooth(top) * (prev_ref[2] * scale)
    x_ref[MAIN + LEV : Q, :] = lon_smooth(low) * (next_ref[2] * scale)
    x_ref[Q:, :] = jnp.zeros((256 - Q, COLS), jnp.float32)
    for half, xt in enumerate((xt_lo, xt_hi)):
        xt[8 : 8 + COLS, :] = x_ref[128 * half : 128 * (half + 1), :].T
        xt[7:8, :] = xt[7 + COLS : 8 + COLS, :]
        xt[8 + COLS : 9 + COLS, :] = xt[8:9, :]
    flat[:, :, FRAME * Q :] = jnp.zeros((2, CHIPS, CHUNK - FRAME * Q), jnp.float32)
    for core in range(2):
        for c in range(FRAME):
            rows = pl.ds(7 + c + BLOCK * core, CHIPS, stride=2 * BLOCK)
            flat[core, :, c * Q : c * Q + 128] = xt_lo[rows, :]
            flat[core, :, c * Q + 128 : (c + 1) * Q] = xt_hi[rows, :][:, : Q - 128]
    first = spot_ref[0:1, :128] == 0.0
    for t in range(TILES):
        even = flat[0, :, 128 * t : 128 * (t + 1)]
        odd = flat[1, :, 128 * t : 128 * (t + 1)]
        keep_ref[pl.ds(t, CHIPS, stride=TILES), :] = jnp.where(first, even, odd)
        send_ref[pl.ds(t, CHIPS, stride=TILES), :] = jnp.where(first, odd, even)
    send_ref[PAIR:, :] = sides_ref[...]


def pair_kernel(keep_ref, got_ref, out_ref):
    out_ref[...] = keep_ref[...] + got_ref[:PAIR, :]


def split_dot(x, pick, dim):
    total = None
    for _ in range(3):
        part = x.astype(jnp.bfloat16)
        x = x - part.astype(jnp.float32)
        got = lax.dot_general(part, pick, (((1,), (dim,)), ((), ())), preferred_element_type=jnp.float32)
        total = got if total is None else total + got
    return total


def tile_kernel(spot_ref, g_ref, near_ref, far_ref, bg_ref, lat_ref, obs_ref, adv_ref, own_ref, edge_ref, flat):
    for t in range(TILES):
        part = g_ref[pl.ds(t, CHIPS, stride=TILES), :]
        flat[0:1, 128 * t : 128 * (t + 1)] = jnp.sum(part, axis=0, keepdims=True)
    first = spot_ref[0:1, :FINE_R] == 0.0
    near, far = near_ref[...], far_ref[...]
    ground = [jnp.where(first, far, near)] + [bg_ref[j] for j in range(FINE_C)] + [jnp.where(first, near, far)]
    q = lax.broadcasted_iota(jnp.int32, (1, Q), 1)
    spot = jnp.where(q < MAIN, (q & 15) + 1, jnp.where(q < MAIN + LEV, 0, ROWS + 1))
    level = jnp.where(q < MAIN, q >> 4, jnp.where(q < MAIN + LEV, q - MAIN, q - MAIN - LEV))
    mask = lax.broadcasted_iota(jnp.int32, (LPAD, Q), 0) == level
    low = lat_ref[:, 0:1] + 1.0
    weight = lat_ref[:, 1:2]

    def table(place):
        place = place.astype(jnp.float32)
        return jnp.where(place == low, 1.0 - weight, 0.0) + jnp.where(place == low + 1.0, weight, 0.0)

    lat = table(spot)
    spread = [jnp.where(mask, flat[0:1, c * Q : (c + 1) * Q], 0.0) for c in range(FRAME)]
    lat_rows = lax.dot_general(jnp.concatenate(spread, axis=0), lat, (((1,), (1,)), ((), ())), precision=highest,
                               preferred_element_type=jnp.float32).reshape(FRAME, LPAD, FINE_R)
    state = []
    for j in range(-1, FINE_C + 1):
        lo, f = interp(j)
        state.append((1.0 - f) * lat_rows[lo] + f * lat_rows[lo + 1] + ground[j + 1])
    slope = [0.5 * (state[j + 2] - state[j]) for j in range(FINE_C)]
    model = [state[j + 1] - advect_rate * state[j + 1] * slope[j] for j in range(FINE_C)]
    for j in range(FINE_C):
        adv_ref[j] = model[j]
    value = obs_ref[0:LPAD, :]
    precision = obs_ref[LPAD : LPAD + 1, :]
    row = obs_ref[LPAD + 1 : LPAD + 2, :]
    col = obs_ref[LPAD + 2 : LPAD + 3, :]
    fine_row = lax.broadcasted_iota(jnp.int32, (FINE_R, NOBS), 0).astype(jnp.float32)
    pick_row = jnp.where(fine_row == row, 1.0, 0.0).astype(jnp.bfloat16)
    pick_col = [jnp.where(col == float(j), 1.0, 0.0) for j in range(FINE_C)]
    seen = split_dot(jnp.concatenate(model, axis=0), pick_row, 0).reshape(FINE_C, LPAD, NOBS)
    observed = sum(pick_col[j] * seen[j] for j in range(FINE_C))
    weighted = precision * (observed - value)
    back = jnp.concatenate([pick_col[j] * weighted for j in range(FINE_C)], axis=0)
    cot = split_dot(back, pick_row, 1).reshape(FINE_C, LPAD, FINE_R)
    half_rate = 0.5 * advect_rate
    flux = [half_rate * state[j + 1] * cot[j] for j in range(FINE_C)]
    total = [None] * FRAME
    for j in range(-1, FINE_C + 1):
        adj = None
        if 0 <= j < FINE_C:
            adj = cot[j] - advect_rate * cot[j] * slope[j]
        if j + 1 < FINE_C:
            adj = flux[j + 1] if adj is None else adj + flux[j + 1]
        if j - 1 >= 0:
            adj = -flux[j - 1] if adj is None else adj - flux[j - 1]
        lo, f = interp(j)
        for c, w in ((lo, 1.0 - f), (lo + 1, f)):
            if w:
                total[c] = w * adj if total[c] is None else total[c] + w * adj
    coarse = jnp.concatenate(total, axis=0)

    def to_coarse(lat, ref):
        wide = jnp.dot(coarse, lat, precision=highest, preferred_element_type=jnp.float32).reshape(FRAME, LPAD, Q)
        for c in range(FRAME):
            flat[0:1, c * Q : (c + 1) * Q] = jnp.sum(jnp.where(mask, wide[c], 0.0), axis=0, keepdims=True)
        for t in range(TILES):
            ref[t : t + 1, :] = flat[0:1, 128 * t : 128 * (t + 1)]

    to_coarse(lat, own_ref)
    to_coarse(table(jnp.where(spot < 2, spot + ROWS, spot - ROWS)), edge_ref)


def share_kernel(own_ref, prev_ref, next_ref, out_ref):
    shape = (TILES, 128)
    q = lax.rem(lax.broadcasted_iota(jnp.int32, shape, 0) * 128 + lax.broadcasted_iota(jnp.int32, shape, 1), Q)
    row = q & 15
    inner = q < MAIN
    from_prev = (inner & (row == 0)) | ((q >= MAIN) & (q < MAIN + LEV))
    from_next = (inner & (row == ROWS - 1)) | (q >= MAIN + LEV)
    total = own_ref[...] + jnp.where(from_prev, prev_ref[...], 0.0) + jnp.where(from_next, next_ref[...], 0.0)
    for m in range(CHIPS):
        out_ref[TILES * m : TILES * (m + 1), :] = total


def gradient_kernel(scale, g_ref, ens_ref, prev_ref, next_ref, out_ref, pad, xt_lo, xt_hi, flat):
    for core in range(2):
        for t in range(TILES):
            flat[core, :, 128 * t : 128 * (t + 1)] = g_ref[pl.ds(core * CHIPS * TILES + t, CHIPS, stride=TILES), :]
    slots = [[flat[core, :, c * Q : (c + 1) * Q] for c in range(FRAME)] for core in range(2)]
    even, odd = slots
    even_first = even[1] + pltpu.roll(odd[FRAME - 1], 1, 0)
    even_last = even[BLOCK] + odd[0]
    odd_first = odd[1] + even[FRAME - 1]
    odd_last = odd[BLOCK] + pltpu.roll(even[0], CHIPS - 1, 0)
    even[1], even[BLOCK], odd[1], odd[BLOCK] = even_first, even_last, odd_first, odd_last
    for core in range(2):
        for c in range(1, BLOCK + 1):
            rows = pl.ds(c - 1 + BLOCK * core, CHIPS, stride=2 * BLOCK)
            xt_lo[rows, :] = slots[core][c][:, :128]
            xt_hi[rows, : Q - 128] = slots[core][c][:, 128:]
    lo = xt_lo[...].T * scale
    hi = xt_hi[...].T * scale
    field = jnp.concatenate([lo, hi[: MAIN - 128, :]], axis=0).reshape(LEV, ROWS, COLS) * ens_ref[...].astype(jnp.float32)
    pad[:, 8:24, :] = field
    pad[:, 7, :] = hi[MAIN - 128 : MAIN - 128 + LEV, :] * prev_ref[2]
    pad[:, 24, :] = hi[MAIN - 128 + LEV : Q - 128, :] * next_ref[2]
    out_ref[...] = lon_smooth(0.25 * pad[:, 7:23, :] + 0.5 * field + 0.25 * pad[:, 9:25, :])


def call(kernel, out, scratch, *args, hbm=False, sems=()):
    def spec(x):
        return pl.BlockSpec(memory_space=pltpu.SMEM if x.dtype == jnp.int32 else pltpu.VMEM)

    return pl.pallas_call(
        kernel,
        out_shape=out,
        in_specs=[pl.BlockSpec(memory_space=pltpu.HBM) if hbm else spec(x) for x in args],
        out_specs=jax.tree.map(spec, out),
        scratch_shapes=[pltpu.VMEM(shape, jnp.float32) for shape in scratch] + list(sems),
        compiler_params=pltpu.CompilerParams(vmem_limit_bytes=40 * 1024 * 1024),
    )(*args)


def f32(*shape):
    return jax.ShapeDtypeStruct(shape, jnp.float32)


def both_ways(up_value, down_value, axis, size, wrap):
    up = [(i, (i + 1) % size) for i in range(size if wrap else size - 1)]
    down = [(j, i) for i, j in up]
    return lax.ppermute(up_value, axis, up), lax.ppermute(down_value, axis, down)


def exchange(flat, tiles):
    parts = lax.all_to_all(flat.reshape(CHIPS, 1, tiles * 128), "chip", 0, 0, tiled=True)
    return parts.reshape(CHIPS * tiles, 128)


def shards(ensemble, alpha, lat_lower, lat_weight, background, obs_cell, obs_value, obs_precision):
    scale = 1.0 / math.sqrt(2 * CHIPS - 1)
    spot = jnp.broadcast_to(lax.axis_index("core").astype(jnp.float32), (1, COLS))
    last, first, alf, ens = call(
        halo_kernel,
        (f32(3, LEV, COLS), f32(3, LEV, COLS), f32(LEV, ROWS, COLS), jax.ShapeDtypeStruct((LEV, ROWS, COLS), jnp.bfloat16)),
        [], pltpu.with_memory_space_constraint(alpha[0], pltpu.HBM), pltpu.with_memory_space_constraint(ensemble[0], pltpu.HBM), hbm=True, sems=[pltpu.SemaphoreType.DMA((2,))],
    )
    before, after = both_ways(last, first, "band", BANDS, False)

    grid = background.reshape(LEV, FINE_R, FINE_C).transpose(2, 0, 1)
    first_core = lax.axis_index("core") == 0
    sides = jnp.where(first_core, grid[FINE_C - 1], grid[0])
    sides = jnp.pad(sides, ((0, LPAD - LEV), (0, 128 - FINE_R)))
    far = jnp.where(first_core, grid[0], grid[FINE_C - 1])
    size = 2 * CHIPS
    far = lax.ppermute(far, ("chip", "core"), [(i, (i + (1 if i % 2 else size - 1)) % size) for i in range(size)])
    far = jnp.pad(far, ((0, LPAD - LEV), (0, 0)))
    ground = jnp.pad(grid, ((0, 0), (0, LPAD - LEV), (0, 0)))
    obs = jnp.concatenate(
        [jnp.pad(obs_value[:, 0, :], ((0, LPAD - LEV), (0, 0))), obs_precision, (obs_cell // FINE_C).astype(jnp.float32),
         (obs_cell % FINE_C).astype(jnp.float32), jnp.zeros((24 - LPAD - 3, NOBS), jnp.float32)], axis=0)
    lat = jnp.stack([lat_lower.astype(jnp.float32), lat_weight], axis=1)
    before, after, ground, sides, obs, lat = lax.optimization_barrier((before, after, ground, sides, obs, lat))

    keep, send = call(
        functools.partial(product_kernel, scale),
        (f32(PAIR, 128), f32(PAIR + LPAD, 128)),
        [(LEV, 32, COLS), (256, COLS), (COLS + 16, 128), (COLS + 16, 128), (2, CHIPS, CHUNK)],
        spot, alf, ens, before, after, sides,
    )
    got = lax.ppermute(send, "core", [(0, 1), (1, 0)])
    gathered = exchange(call(pair_kernel, f32(PAIR, 128), [], keep, got), TILES)
    moved, own, edge = call(
        tile_kernel,
        (f32(FINE_C, LPAD, FINE_R), f32(TILES, 128), f32(TILES, 128)),
        [(8, CHUNK)],
        spot, gathered, got[PAIR:, :FINE_R], far, ground, lat, obs,
    )
    from_prev, from_next = both_ways(edge, edge, "band", BANDS, False)
    shared = call(share_kernel, f32(CHIPS * TILES, 128), [], own, from_prev, from_next)
    everyone = lax.all_gather(exchange(shared, TILES), "core", axis=0, tiled=True)
    gradient = call(
        functools.partial(gradient_kernel, scale),
        f32(LEV, ROWS, COLS),
        [(LEV, 32, COLS), (COLS, 128), (COLS, 128), (2, CHIPS, CHUNK)],
        everyone, ens, before, after,
    )
    advected = moved[:, :LEV].transpose(1, 2, 0).reshape(LEV, 1, FINE_R * FINE_C)
    return (advected, gradient[None])


def solution(mesh):
    member = ("chip", "core")
    tile = ("band", "chip", "core")
    return jax.shard_map(
        shards,
        mesh=jax.sharding.Mesh(mesh.devices.reshape(CHIPS, 2, BANDS), ("chip", "core", "band")),
        in_specs=(
            P(member, None, "band", None),
            P(member, None, "band", None),
            P("band"),
            P("band"),
            P(None, tile, None),
            P(tile, None),
            P(None, tile, None),
            P(tile, None),
        ),
        out_specs=(P(None, tile, None), P(member, None, "band", None)),
        check_vma=False,
    )
```

```python
import functools
import math

import jax
import jax.numpy as jnp
from jax import lax
from jax.experimental import pallas as pl
from jax.experimental.pallas import tpu as pltpu
from jax.sharding import PartitionSpec as P

LEV = 12
LPAD = 16
ROWS = 16
COLS = 512
CHIPS = 32
BANDS = 8
BLOCK = 8
FRAME = BLOCK + 2
FINE_R = 48
FINE_C = 24
NOBS = 256
MAIN = LEV * ROWS
Q = MAIN + 2 * LEV
TILES = 17
CHUNK = TILES * 128
PAIR = CHIPS * TILES

advect_rate = 0.25
highest = lax.Precision.HIGHEST


def lon_smooth(x):
    axis = x.ndim - 1
    return 0.25 * pltpu.roll(x, 1, axis) + 0.5 * x + 0.25 * pltpu.roll(x, COLS - 1, axis)


def interp(j):
    n = 2 * j + 4
    return n // 6, (n % 6) / 6.0


def halo_kernel(alpha_hbm, ens_hbm, last_ref, first_ref, alpha_ref, ens_ref, sems):
    copies = [pltpu.make_async_copy(alpha_hbm, alpha_ref, sems.at[0]), pltpu.make_async_copy(ens_hbm, ens_ref, sems.at[1])]
    for copy in copies:
        copy.start()
    for copy in copies:
        copy.wait()
    last_ref[0] = alpha_ref[:, ROWS - 2, :]
    last_ref[1] = alpha_ref[:, ROWS - 1, :]
    last_ref[2] = ens_ref[:, ROWS - 1, :].astype(jnp.float32)
    first_ref[0] = alpha_ref[:, 0, :]
    first_ref[1] = alpha_ref[:, 1, :]
    first_ref[2] = ens_ref[:, 0, :].astype(jnp.float32)


def product_kernel(scale, spot_ref, alpha_ref, ens_ref, prev_ref, next_ref, sides_ref, keep_ref, send_ref, pad, x_ref, xt_lo, xt_hi, flat):
    pad[:, 8:24, :] = alpha_ref[...]
    pad[:, 7, :] = prev_ref[1]
    pad[:, 24, :] = next_ref[0]
    body = 0.25 * pad[:, 7:23, :] + 0.5 * alpha_ref[...] + 0.25 * pad[:, 9:25, :]
    body = lon_smooth(body) * (ens_ref[...].astype(jnp.float32) * scale)
    top = 0.25 * prev_ref[0] + 0.5 * prev_ref[1] + 0.25 * alpha_ref[:, 0, :]
    low = 0.25 * alpha_ref[:, ROWS - 1, :] + 0.5 * next_ref[0] + 0.25 * next_ref[1]
    x_ref[:MAIN, :] = body.reshape(MAIN, COLS)
    x_ref[MAIN : MAIN + LEV, :] = lon_smooth(top) * (prev_ref[2] * scale)
    x_ref[MAIN + LEV : Q, :] = lon_smooth(low) * (next_ref[2] * scale)
    x_ref[Q:, :] = jnp.zeros((256 - Q, COLS), jnp.float32)
    for half, xt in enumerate((xt_lo, xt_hi)):
        xt[8 : 8 + COLS, :] = x_ref[128 * half : 128 * (half + 1), :].T
        xt[7:8, :] = xt[7 + COLS : 8 + COLS, :]
        xt[8 + COLS : 9 + COLS, :] = xt[8:9, :]
    flat[:, :, FRAME * Q :] = jnp.zeros((2, CHIPS, CHUNK - FRAME * Q), jnp.float32)
    for core in range(2):
        for c in range(FRAME):
            rows = pl.ds(7 + c + BLOCK * core, CHIPS, stride=2 * BLOCK)
            flat[core, :, c * Q : c * Q + 128] = xt_lo[rows, :]
            flat[core, :, c * Q + 128 : (c + 1) * Q] = xt_hi[rows, :][:, : Q - 128]
    first = spot_ref[0:1, :128] == 0.0
    for t in range(TILES):
        even = flat[0, :, 128 * t : 128 * (t + 1)]
        odd = flat[1, :, 128 * t : 128 * (t + 1)]
        keep_ref[pl.ds(t, CHIPS, stride=TILES), :] = jnp.where(first, even, odd)
        send_ref[pl.ds(t, CHIPS, stride=TILES), :] = jnp.where(first, odd, even)
    send_ref[PAIR:, :] = sides_ref[...]


def pair_kernel(spot_ref, keep_ref, both_ref, out_ref, near_ref):
    first = spot_ref[0:1, :128] == 0.0
    out_ref[...] = keep_ref[...] + jnp.where(first, both_ref[PAIR + LPAD : 2 * PAIR + LPAD, :], both_ref[:PAIR, :])
    near_ref[...] = jnp.where(first, both_ref[2 * PAIR + LPAD :, :], both_ref[PAIR : PAIR + LPAD, :])


def split_dot(x, pick, dim):
    total = None
    for _ in range(3):
        part = x.astype(jnp.bfloat16)
        x = x - part.astype(jnp.float32)
        got = lax.dot_general(part, pick, (((1,), (dim,)), ((), ())), preferred_element_type=jnp.float32)
        total = got if total is None else total + got
    return total


def tile_kernel(spot_ref, g_ref, near_ref, far_ref, bg_ref, lat_ref, obs_ref, adv_ref, own_ref, edge_ref, flat):
    for t in range(TILES):
        part = g_ref[pl.ds(t, CHIPS, stride=TILES), :]
        flat[0:1, 128 * t : 128 * (t + 1)] = jnp.sum(part, axis=0, keepdims=True)
    first = spot_ref[0:1, :FINE_R] == 0.0
    near, far = near_ref[:, :FINE_R], far_ref[...]
    ground = [jnp.where(first, far, near)] + [bg_ref[j] for j in range(FINE_C)] + [jnp.where(first, near, far)]
    q = lax.broadcasted_iota(jnp.int32, (1, Q), 1)
    spot = jnp.where(q < MAIN, (q & 15) + 1, jnp.where(q < MAIN + LEV, 0, ROWS + 1))
    level = jnp.where(q < MAIN, q >> 4, jnp.where(q < MAIN + LEV, q - MAIN, q - MAIN - LEV))
    mask = lax.broadcasted_iota(jnp.int32, (LPAD, Q), 0) == level
    low = lat_ref[:, 0:1] + 1.0
    weight = lat_ref[:, 1:2]

    def table(place):
        place = place.astype(jnp.float32)
        return jnp.where(place == low, 1.0 - weight, 0.0) + jnp.where(place == low + 1.0, weight, 0.0)

    lat = table(spot)
    spread = [jnp.where(mask, flat[0:1, c * Q : (c + 1) * Q], 0.0) for c in range(FRAME)]
    lat_rows = lax.dot_general(jnp.concatenate(spread, axis=0), lat, (((1,), (1,)), ((), ())), precision=highest,
                               preferred_element_type=jnp.float32).reshape(FRAME, LPAD, FINE_R)
    state = []
    for j in range(-1, FINE_C + 1):
        lo, f = interp(j)
        state.append((1.0 - f) * lat_rows[lo] + f * lat_rows[lo + 1] + ground[j + 1])
    slope = [0.5 * (state[j + 2] - state[j]) for j in range(FINE_C)]
    model = [state[j + 1] - advect_rate * state[j + 1] * slope[j] for j in range(FINE_C)]
    for j in range(FINE_C):
        adv_ref[j] = model[j]
    value = obs_ref[0:LPAD, :]
    precision = obs_ref[LPAD : LPAD + 1, :]
    row = obs_ref[LPAD + 1 : LPAD + 2, :]
    col = obs_ref[LPAD + 2 : LPAD + 3, :]
    fine_row = lax.broadcasted_iota(jnp.int32, (FINE_R, NOBS), 0).astype(jnp.float32)
    pick_row = jnp.where(fine_row == row, 1.0, 0.0).astype(jnp.bfloat16)
    pick_col = [jnp.where(col == float(j), 1.0, 0.0) for j in range(FINE_C)]
    seen = split_dot(jnp.concatenate(model, axis=0), pick_row, 0).reshape(FINE_C, LPAD, NOBS)
    observed = sum(pick_col[j] * seen[j] for j in range(FINE_C))
    weighted = precision * (observed - value)
    back = jnp.concatenate([pick_col[j] * weighted for j in range(FINE_C)], axis=0)
    cot = split_dot(back, pick_row, 1).reshape(FINE_C, LPAD, FINE_R)
    half_rate = 0.5 * advect_rate
    flux = [half_rate * state[j + 1] * cot[j] for j in range(FINE_C)]
    total = [None] * FRAME
    for j in range(-1, FINE_C + 1):
        adj = None
        if 0 <= j < FINE_C:
            adj = cot[j] - advect_rate * cot[j] * slope[j]
        if j + 1 < FINE_C:
            adj = flux[j + 1] if adj is None else adj + flux[j + 1]
        if j - 1 >= 0:
            adj = -flux[j - 1] if adj is None else adj - flux[j - 1]
        lo, f = interp(j)
        for c, w in ((lo, 1.0 - f), (lo + 1, f)):
            if w:
                total[c] = w * adj if total[c] is None else total[c] + w * adj
    coarse = jnp.concatenate(total, axis=0)

    def to_coarse(lat, ref):
        wide = jnp.dot(coarse, lat, precision=highest, preferred_element_type=jnp.float32).reshape(FRAME, LPAD, Q)
        for c in range(FRAME):
            flat[0:1, c * Q : (c + 1) * Q] = jnp.sum(jnp.where(mask, wide[c], 0.0), axis=0, keepdims=True)
        for t in range(TILES):
            ref[t : t + 1, :] = flat[0:1, 128 * t : 128 * (t + 1)]

    to_coarse(lat, own_ref)
    to_coarse(table(jnp.where(spot < 2, spot + ROWS, spot - ROWS)), edge_ref)


def share_kernel(own_ref, prev_ref, next_ref, out_ref):
    shape = (TILES, 128)
    q = lax.rem(lax.broadcasted_iota(jnp.int32, shape, 0) * 128 + lax.broadcasted_iota(jnp.int32, shape, 1), Q)
    row = q & 15
    inner = q < MAIN
    from_prev = (inner & (row == 0)) | ((q >= MAIN) & (q < MAIN + LEV))
    from_next = (inner & (row == ROWS - 1)) | (q >= MAIN + LEV)
    total = own_ref[...] + jnp.where(from_prev, prev_ref[...], 0.0) + jnp.where(from_next, next_ref[...], 0.0)
    for m in range(CHIPS):
        out_ref[TILES * m : TILES * (m + 1), :] = total


def gradient_kernel(scale, g_ref, ens_ref, prev_ref, next_ref, out_ref, pad, xt_lo, xt_hi, flat):
    for core in range(2):
        for t in range(TILES):
            flat[core, :, 128 * t : 128 * (t + 1)] = g_ref[pl.ds(core * CHIPS * TILES + t, CHIPS, stride=TILES), :]
    slots = [[flat[core, :, c * Q : (c + 1) * Q] for c in range(FRAME)] for core in range(2)]
    even, odd = slots
    even_first = even[1] + pltpu.roll(odd[FRAME - 1], 1, 0)
    even_last = even[BLOCK] + odd[0]
    odd_first = odd[1] + even[FRAME - 1]
    odd_last = odd[BLOCK] + pltpu.roll(even[0], CHIPS - 1, 0)
    even[1], even[BLOCK], odd[1], odd[BLOCK] = even_first, even_last, odd_first, odd_last
    for core in range(2):
        for c in range(1, BLOCK + 1):
            rows = pl.ds(c - 1 + BLOCK * core, CHIPS, stride=2 * BLOCK)
            xt_lo[rows, :] = slots[core][c][:, :128]
            xt_hi[rows, : Q - 128] = slots[core][c][:, 128:]
    lo = xt_lo[...].T * scale
    hi = xt_hi[...].T * scale
    field = jnp.concatenate([lo, hi[: MAIN - 128, :]], axis=0).reshape(LEV, ROWS, COLS) * ens_ref[...].astype(jnp.float32)
    pad[:, 8:24, :] = field
    pad[:, 7, :] = hi[MAIN - 128 : MAIN - 128 + LEV, :] * prev_ref[2]
    pad[:, 24, :] = hi[MAIN - 128 + LEV : Q - 128, :] * next_ref[2]
    out_ref[...] = lon_smooth(0.25 * pad[:, 7:23, :] + 0.5 * field + 0.25 * pad[:, 9:25, :])


def call(kernel, out, scratch, *args, hbm=False, sems=()):
    def spec(x):
        return pl.BlockSpec(memory_space=pltpu.SMEM if x.dtype == jnp.int32 else pltpu.VMEM)

    return pl.pallas_call(
        kernel,
        out_shape=out,
        in_specs=[pl.BlockSpec(memory_space=pltpu.HBM) if hbm else spec(x) for x in args],
        out_specs=jax.tree.map(spec, out),
        scratch_shapes=[pltpu.VMEM(shape, jnp.float32) for shape in scratch] + list(sems),
        compiler_params=pltpu.CompilerParams(vmem_limit_bytes=40 * 1024 * 1024),
    )(*args)


def f32(*shape):
    return jax.ShapeDtypeStruct(shape, jnp.float32)


def both_ways(up_value, down_value, axis, size, wrap):
    up = [(i, (i + 1) % size) for i in range(size if wrap else size - 1)]
    down = [(j, i) for i, j in up]
    return lax.ppermute(up_value, axis, up), lax.ppermute(down_value, axis, down)


def exchange(flat, tiles):
    parts = lax.all_to_all(flat.reshape(CHIPS, 1, tiles * 128), "chip", 0, 0, tiled=True)
    return parts.reshape(CHIPS * tiles, 128)


def shards(ensemble, alpha, lat_lower, lat_weight, background, obs_cell, obs_value, obs_precision):
    scale = 1.0 / math.sqrt(2 * CHIPS - 1)
    spot = jnp.broadcast_to(lax.axis_index("core").astype(jnp.float32), (1, COLS))
    last, first, alf, ens = call(
        halo_kernel,
        (f32(3, LEV, COLS), f32(3, LEV, COLS), f32(LEV, ROWS, COLS), jax.ShapeDtypeStruct((LEV, ROWS, COLS), jnp.bfloat16)),
        [], pltpu.with_memory_space_constraint(alpha[0], pltpu.HBM), pltpu.with_memory_space_constraint(ensemble[0], pltpu.HBM), hbm=True, sems=[pltpu.SemaphoreType.DMA((2,))],
    )
    before, after = both_ways(last, first, "band", BANDS, False)

    grid = background.reshape(LEV, FINE_R, FINE_C).transpose(2, 0, 1)
    first_core = lax.axis_index("core") == 0
    sides = jnp.where(first_core, grid[FINE_C - 1], grid[0])
    sides = jnp.pad(sides, ((0, LPAD - LEV), (0, 128 - FINE_R)))
    far = jnp.where(first_core, grid[0], grid[FINE_C - 1])
    size = 2 * CHIPS
    far = lax.ppermute(far, ("chip", "core"), [(i, (i + (1 if i % 2 else size - 1)) % size) for i in range(size)])
    far = jnp.pad(far, ((0, LPAD - LEV), (0, 0)))
    ground = jnp.pad(grid, ((0, 0), (0, LPAD - LEV), (0, 0)))
    obs = jnp.concatenate(
        [jnp.pad(obs_value[:, 0, :], ((0, LPAD - LEV), (0, 0))), obs_precision, (obs_cell // FINE_C).astype(jnp.float32),
         (obs_cell % FINE_C).astype(jnp.float32), jnp.zeros((24 - LPAD - 3, NOBS), jnp.float32)], axis=0)
    lat = jnp.stack([lat_lower.astype(jnp.float32), lat_weight], axis=1)
    before, after, ground, sides, obs, lat = lax.optimization_barrier((before, after, ground, sides, obs, lat))

    keep, send = call(
        functools.partial(product_kernel, scale),
        (f32(PAIR, 128), f32(PAIR + LPAD, 128)),
        [(LEV, 32, COLS), (256, COLS), (COLS + 16, 128), (COLS + 16, 128), (2, CHIPS, CHUNK)],
        spot, alf, ens, before, after, sides,
    )
    both = lax.all_gather(send, "core", axis=0, tiled=True)
    paired, near = call(pair_kernel, (f32(PAIR, 128), f32(LPAD, 128)), [], spot, keep, both)
    gathered = exchange(paired, TILES)
    moved, own, edge = call(
        tile_kernel,
        (f32(FINE_C, LPAD, FINE_R), f32(TILES, 128), f32(TILES, 128)),
        [(8, CHUNK)],
        spot, gathered, near, far, ground, lat, obs,
    )
    from_prev, from_next = both_ways(edge, edge, "band", BANDS, False)
    shared = call(share_kernel, f32(CHIPS * TILES, 128), [], own, from_prev, from_next)
    everyone = lax.all_gather(exchange(shared, TILES), "core", axis=0, tiled=True)
    gradient = call(
        functools.partial(gradient_kernel, scale),
        f32(LEV, ROWS, COLS),
        [(LEV, 32, COLS), (COLS, 128), (COLS, 128), (2, CHIPS, CHUNK)],
        everyone, ens, before, after,
    )
    advected = moved[:, :LEV].transpose(1, 2, 0).reshape(LEV, 1, FINE_R * FINE_C)
    return (advected, gradient[None])


def solution(mesh):
    member = ("chip", "core")
    tile = ("band", "chip", "core")
    return jax.shard_map(
        shards,
        mesh=jax.sharding.Mesh(mesh.devices.reshape(CHIPS, 2, BANDS), ("chip", "core", "band")),
        in_specs=(
            P(member, None, "band", None),
            P(member, None, "band", None),
            P("band"),
            P("band"),
            P(None, tile, None),
            P(tile, None),
            P(None, tile, None),
            P(tile, None),
        ),
        out_specs=(P(None, tile, None), P(member, None, "band", None)),
        check_vma=False,
    )
```

```python
import functools
import math

import jax
import jax.numpy as jnp
from jax import lax
from jax.experimental import pallas as pl
from jax.experimental.pallas import tpu as pltpu
from jax.sharding import PartitionSpec as P

LEV = 12
LPAD = 16
ROWS = 16
COLS = 512
CHIPS = 32
BANDS = 8
BLOCK = 8
FRAME = BLOCK + 2
FINE_R = 48
FINE_C = 24
NOBS = 256
MAIN = LEV * ROWS
Q = MAIN + 2 * LEV
TILES = 17
CHUNK = TILES * 128
PAIR = CHIPS * TILES

advect_rate = 0.25
highest = lax.Precision.HIGHEST


def lon_smooth(x):
    axis = x.ndim - 1
    return 0.25 * pltpu.roll(x, 1, axis) + 0.5 * x + 0.25 * pltpu.roll(x, COLS - 1, axis)


def interp(j):
    n = 2 * j + 4
    return n // 6, (n % 6) / 6.0


def halo_kernel(alpha_hbm, ens_hbm, last_ref, first_ref, alpha_ref, ens_ref, sems):
    copies = [pltpu.make_async_copy(alpha_hbm, alpha_ref, sems.at[0]), pltpu.make_async_copy(ens_hbm, ens_ref, sems.at[1])]
    for copy in copies:
        copy.start()
    for copy in copies:
        copy.wait()
    last_ref[0] = alpha_ref[:, ROWS - 2, :]
    last_ref[1] = alpha_ref[:, ROWS - 1, :]
    last_ref[2] = ens_ref[:, ROWS - 1, :].astype(jnp.float32)
    first_ref[0] = alpha_ref[:, 0, :]
    first_ref[1] = alpha_ref[:, 1, :]
    first_ref[2] = ens_ref[:, 0, :].astype(jnp.float32)


def product_kernel(scale, spot_ref, alpha_ref, ens_ref, prev_ref, next_ref, sides_ref, keep_ref, send_ref, pad, x_ref, xt_lo, xt_hi, flat):
    pad[:, 8:24, :] = alpha_ref[...]
    pad[:, 7, :] = prev_ref[1]
    pad[:, 24, :] = next_ref[0]
    body = 0.25 * pad[:, 7:23, :] + 0.5 * alpha_ref[...] + 0.25 * pad[:, 9:25, :]
    body = lon_smooth(body) * (ens_ref[...].astype(jnp.float32) * scale)
    top = 0.25 * prev_ref[0] + 0.5 * prev_ref[1] + 0.25 * alpha_ref[:, 0, :]
    low = 0.25 * alpha_ref[:, ROWS - 1, :] + 0.5 * next_ref[0] + 0.25 * next_ref[1]
    x_ref[:MAIN, :] = body.reshape(MAIN, COLS)
    x_ref[MAIN : MAIN + LEV, :] = lon_smooth(top) * (prev_ref[2] * scale)
    x_ref[MAIN + LEV : Q, :] = lon_smooth(low) * (next_ref[2] * scale)
    x_ref[Q:, :] = jnp.zeros((256 - Q, COLS), jnp.float32)
    for half, xt in enumerate((xt_lo, xt_hi)):
        xt[8 : 8 + COLS, :] = x_ref[128 * half : 128 * (half + 1), :].T
        xt[7:8, :] = xt[7 + COLS : 8 + COLS, :]
        xt[8 + COLS : 9 + COLS, :] = xt[8:9, :]
    flat[:, :, FRAME * Q :] = jnp.zeros((2, CHIPS, CHUNK - FRAME * Q), jnp.float32)
    for core in range(2):
        for c in range(FRAME):
            rows = pl.ds(7 + c + BLOCK * core, CHIPS, stride=2 * BLOCK)
            flat[core, :, c * Q : c * Q + 128] = xt_lo[rows, :]
            flat[core, :, c * Q + 128 : (c + 1) * Q] = xt_hi[rows, :][:, : Q - 128]
    first = spot_ref[0:1, :128] == 0.0
    for t in range(TILES):
        even = flat[0, :, 128 * t : 128 * (t + 1)]
        odd = flat[1, :, 128 * t : 128 * (t + 1)]
        keep_ref[pl.ds(t, CHIPS, stride=TILES), :] = jnp.where(first, even, odd)
        send_ref[pl.ds(t, CHIPS, stride=TILES), :] = jnp.where(first, odd, even)
    send_ref[PAIR:, :] = sides_ref[...]


def pair_kernel(spot_ref, keep_ref, both_ref, out_ref, near_ref):
    first = spot_ref[0:1, :128] == 0.0
    out_ref[...] = keep_ref[...] + jnp.where(first, both_ref[PAIR + LPAD : 2 * PAIR + LPAD, :], both_ref[:PAIR, :])
    near_ref[...] = jnp.where(first, both_ref[2 * PAIR + LPAD :, :], both_ref[PAIR : PAIR + LPAD, :])


def split_dot(x, pick, dim):
    total = None
    for _ in range(3):
        part = x.astype(jnp.bfloat16)
        x = x - part.astype(jnp.float32)
        got = lax.dot_general(part, pick, (((1,), (dim,)), ((), ())), preferred_element_type=jnp.float32)
        total = got if total is None else total + got
    return total


def places(lat_ref):
    q = lax.broadcasted_iota(jnp.int32, (1, Q), 1)
    spot = jnp.where(q < MAIN, (q & 15) + 1, jnp.where(q < MAIN + LEV, 0, ROWS + 1))
    level = jnp.where(q < MAIN, q >> 4, jnp.where(q < MAIN + LEV, q - MAIN, q - MAIN - LEV))
    mask = lax.broadcasted_iota(jnp.int32, (LPAD, Q), 0) == level
    low = lat_ref[:, 0:1] + 1.0
    weight = lat_ref[:, 1:2]

    def table(place):
        place = place.astype(jnp.float32)
        return jnp.where(place == low, 1.0 - weight, 0.0) + jnp.where(place == low + 1.0, weight, 0.0)

    return spot, mask, table


def to_coarse(coarse, lat, mask, flat, ref):
    wide = jnp.dot(coarse, lat, precision=highest, preferred_element_type=jnp.float32).reshape(FRAME, LPAD, Q)
    for c in range(FRAME):
        flat[0:1, c * Q : (c + 1) * Q] = jnp.sum(jnp.where(mask, wide[c], 0.0), axis=0, keepdims=True)
    for t in range(TILES):
        ref[t : t + 1, :] = flat[0:1, 128 * t : 128 * (t + 1)]


def own_kernel(coarse_ref, lat_ref, own_ref, flat):
    flat[...] = jnp.zeros_like(flat)
    spot, mask, table = places(lat_ref)
    to_coarse(coarse_ref[...], table(spot), mask, flat, own_ref)


def tile_kernel(spot_ref, g_ref, near_ref, far_ref, bg_ref, lat_ref, obs_ref, adv_ref, coarse_ref, edge_ref, flat):
    for t in range(TILES):
        part = g_ref[pl.ds(t, CHIPS, stride=TILES), :]
        flat[0:1, 128 * t : 128 * (t + 1)] = jnp.sum(part, axis=0, keepdims=True)
    first = spot_ref[0:1, :FINE_R] == 0.0
    near, far = near_ref[:, :FINE_R], far_ref[...]
    ground = [jnp.where(first, far, near)] + [bg_ref[j] for j in range(FINE_C)] + [jnp.where(first, near, far)]
    spot, mask, table = places(lat_ref)
    lat = table(spot)
    spread = [jnp.where(mask, flat[0:1, c * Q : (c + 1) * Q], 0.0) for c in range(FRAME)]
    lat_rows = lax.dot_general(jnp.concatenate(spread, axis=0), lat, (((1,), (1,)), ((), ())), precision=highest,
                               preferred_element_type=jnp.float32).reshape(FRAME, LPAD, FINE_R)
    state = []
    for j in range(-1, FINE_C + 1):
        lo, f = interp(j)
        state.append((1.0 - f) * lat_rows[lo] + f * lat_rows[lo + 1] + ground[j + 1])
    slope = [0.5 * (state[j + 2] - state[j]) for j in range(FINE_C)]
    model = [state[j + 1] - advect_rate * state[j + 1] * slope[j] for j in range(FINE_C)]
    for j in range(FINE_C):
        adv_ref[j] = model[j]
    value = obs_ref[0:LPAD, :]
    precision = obs_ref[LPAD : LPAD + 1, :]
    row = obs_ref[LPAD + 1 : LPAD + 2, :]
    col = obs_ref[LPAD + 2 : LPAD + 3, :]
    fine_row = lax.broadcasted_iota(jnp.int32, (FINE_R, NOBS), 0).astype(jnp.float32)
    pick_row = jnp.where(fine_row == row, 1.0, 0.0).astype(jnp.bfloat16)
    pick_col = [jnp.where(col == float(j), 1.0, 0.0) for j in range(FINE_C)]
    seen = split_dot(jnp.concatenate(model, axis=0), pick_row, 0).reshape(FINE_C, LPAD, NOBS)
    observed = sum(pick_col[j] * seen[j] for j in range(FINE_C))
    weighted = precision * (observed - value)
    back = jnp.concatenate([pick_col[j] * weighted for j in range(FINE_C)], axis=0)
    cot = split_dot(back, pick_row, 1).reshape(FINE_C, LPAD, FINE_R)
    half_rate = 0.5 * advect_rate
    flux = [half_rate * state[j + 1] * cot[j] for j in range(FINE_C)]
    total = [None] * FRAME
    for j in range(-1, FINE_C + 1):
        adj = None
        if 0 <= j < FINE_C:
            adj = cot[j] - advect_rate * cot[j] * slope[j]
        if j + 1 < FINE_C:
            adj = flux[j + 1] if adj is None else adj + flux[j + 1]
        if j - 1 >= 0:
            adj = -flux[j - 1] if adj is None else adj - flux[j - 1]
        lo, f = interp(j)
        for c, w in ((lo, 1.0 - f), (lo + 1, f)):
            if w:
                total[c] = w * adj if total[c] is None else total[c] + w * adj
    coarse = jnp.concatenate(total, axis=0)

    coarse_ref[...] = coarse
    to_coarse(coarse, table(jnp.where(spot < 2, spot + ROWS, spot - ROWS)), mask, flat, edge_ref)


def share_kernel(own_ref, prev_ref, next_ref, out_ref):
    shape = (TILES, 128)
    q = lax.rem(lax.broadcasted_iota(jnp.int32, shape, 0) * 128 + lax.broadcasted_iota(jnp.int32, shape, 1), Q)
    row = q & 15
    inner = q < MAIN
    from_prev = (inner & (row == 0)) | ((q >= MAIN) & (q < MAIN + LEV))
    from_next = (inner & (row == ROWS - 1)) | (q >= MAIN + LEV)
    total = own_ref[...] + jnp.where(from_prev, prev_ref[...], 0.0) + jnp.where(from_next, next_ref[...], 0.0)
    for m in range(CHIPS):
        out_ref[TILES * m : TILES * (m + 1), :] = total


def gradient_kernel(scale, g_ref, ens_ref, prev_ref, next_ref, out_hbm, pad, xt_lo, xt_hi, flat, out_ref, sems):
    for core in range(2):
        for t in range(TILES):
            flat[core, :, 128 * t : 128 * (t + 1)] = g_ref[pl.ds(core * CHIPS * TILES + t, CHIPS, stride=TILES), :]
    slots = [[flat[core, :, c * Q : (c + 1) * Q] for c in range(FRAME)] for core in range(2)]
    even, odd = slots
    even_first = even[1] + pltpu.roll(odd[FRAME - 1], 1, 0)
    even_last = even[BLOCK] + odd[0]
    odd_first = odd[1] + even[FRAME - 1]
    odd_last = odd[BLOCK] + pltpu.roll(even[0], CHIPS - 1, 0)
    even[1], even[BLOCK], odd[1], odd[BLOCK] = even_first, even_last, odd_first, odd_last
    for core in range(2):
        for c in range(1, BLOCK + 1):
            rows = pl.ds(c - 1 + BLOCK * core, CHIPS, stride=2 * BLOCK)
            xt_lo[rows, :] = slots[core][c][:, :128]
            xt_hi[rows, : Q - 128] = slots[core][c][:, 128:]
    lo = xt_lo[...].T * scale
    hi = xt_hi[...].T * scale
    field = jnp.concatenate([lo, hi[: MAIN - 128, :]], axis=0).reshape(LEV, ROWS, COLS) * ens_ref[...].astype(jnp.float32)
    pad[:, 8:24, :] = field
    pad[:, 7, :] = hi[MAIN - 128 : MAIN - 128 + LEV, :] * prev_ref[2]
    pad[:, 24, :] = hi[MAIN - 128 + LEV : Q - 128, :] * next_ref[2]
    copies = []
    for k in range(3):
        lev = slice(4 * k, 4 * (k + 1))
        out_ref[lev] = lon_smooth(0.25 * pad[lev, 7:23, :] + 0.5 * pad[lev, 8:24, :] + 0.25 * pad[lev, 9:25, :])
        copies.append(pltpu.make_async_copy(out_ref.at[lev], out_hbm.at[lev], sems.at[k]))
        copies[k].start()
    for copy in copies:
        copy.wait()


def call(kernel, out, scratch, *args, hbm=False, sems=(), away=False):
    def spec(x):
        return pl.BlockSpec(memory_space=pltpu.SMEM if x.dtype == jnp.int32 else pltpu.VMEM)

    return pl.pallas_call(
        kernel,
        out_shape=out,
        in_specs=[pl.BlockSpec(memory_space=pltpu.HBM) if hbm else spec(x) for x in args],
        out_specs=pl.BlockSpec(memory_space=pl.ANY) if away else jax.tree.map(spec, out),
        scratch_shapes=[pltpu.VMEM(shape, jnp.float32) for shape in scratch] + list(sems),
        compiler_params=pltpu.CompilerParams(vmem_limit_bytes=40 * 1024 * 1024),
    )(*args)


def f32(*shape):
    return jax.ShapeDtypeStruct(shape, jnp.float32)


def both_ways(up_value, down_value, axis, size, wrap):
    up = [(i, (i + 1) % size) for i in range(size if wrap else size - 1)]
    down = [(j, i) for i, j in up]
    return lax.ppermute(up_value, axis, up), lax.ppermute(down_value, axis, down)


def exchange(flat, tiles):
    parts = lax.all_to_all(flat.reshape(CHIPS, 1, tiles * 128), "chip", 0, 0, tiled=True)
    return parts.reshape(CHIPS * tiles, 128)


def shards(ensemble, alpha, lat_lower, lat_weight, background, obs_cell, obs_value, obs_precision):
    scale = 1.0 / math.sqrt(2 * CHIPS - 1)
    spot = jnp.broadcast_to(lax.axis_index("core").astype(jnp.float32), (1, COLS))
    last, first, alf, ens = call(
        halo_kernel,
        (f32(3, LEV, COLS), f32(3, LEV, COLS), f32(LEV, ROWS, COLS), jax.ShapeDtypeStruct((LEV, ROWS, COLS), jnp.bfloat16)),
        [], pltpu.with_memory_space_constraint(alpha[0], pltpu.HBM), pltpu.with_memory_space_constraint(ensemble[0], pltpu.HBM), hbm=True, sems=[pltpu.SemaphoreType.DMA((2,))],
    )
    before, after = both_ways(last, first, "band", BANDS, False)

    grid = background.reshape(LEV, FINE_R, FINE_C).transpose(2, 0, 1)
    first_core = lax.axis_index("core") == 0
    sides = jnp.where(first_core, grid[FINE_C - 1], grid[0])
    sides = jnp.pad(sides, ((0, LPAD - LEV), (0, 128 - FINE_R)))
    far = jnp.where(first_core, grid[0], grid[FINE_C - 1])
    size = 2 * CHIPS
    ground = jnp.pad(grid, ((0, 0), (0, LPAD - LEV), (0, 0)))
    obs = jnp.concatenate(
        [jnp.pad(obs_value[:, 0, :], ((0, LPAD - LEV), (0, 0))), obs_precision, (obs_cell // FINE_C).astype(jnp.float32),
         (obs_cell % FINE_C).astype(jnp.float32), jnp.zeros((24 - LPAD - 3, NOBS), jnp.float32)], axis=0)
    lat = jnp.stack([lat_lower.astype(jnp.float32), lat_weight], axis=1)
    before, after, ground, sides, far = lax.optimization_barrier((before, after, ground, sides, far))

    keep, send = call(
        functools.partial(product_kernel, scale),
        (f32(PAIR, 128), f32(PAIR + LPAD, 128)),
        [(LEV, 32, COLS), (256, COLS), (COLS + 16, 128), (COLS + 16, 128), (2, CHIPS, CHUNK)],
        spot, alf, ens, before, after, sides,
    )
    both = lax.all_gather(send, "core", axis=0, tiled=True)
    paired, near = call(pair_kernel, (f32(PAIR, 128), f32(LPAD, 128)), [], spot, keep, both)
    paired, far = lax.optimization_barrier((paired, far))
    gathered = exchange(paired, TILES)
    far = lax.ppermute(far, ("chip", "core"), [(i, (i + (1 if i % 2 else size - 1)) % size) for i in range(size)])
    far = jnp.pad(far, ((0, LPAD - LEV), (0, 0)))
    moved, coarse, edge = call(
        tile_kernel,
        (f32(FINE_C, LPAD, FINE_R), f32(FRAME * LPAD, FINE_R), f32(TILES, 128)),
        [(8, CHUNK)],
        spot, gathered, near, far, ground, lat, obs,
    )
    from_prev, from_next = both_ways(edge, edge, "band", BANDS, False)
    own = call(own_kernel, f32(TILES, 128), [(8, CHUNK)], coarse, lat)
    shared = call(share_kernel, f32(CHIPS * TILES, 128), [], own, from_prev, from_next)
    everyone = lax.all_gather(exchange(shared, TILES), "core", axis=0, tiled=True)
    gradient = call(
        functools.partial(gradient_kernel, scale),
        f32(LEV, ROWS, COLS),
        [(LEV, 32, COLS), (COLS, 128), (COLS, 128), (2, CHIPS, CHUNK), (LEV, ROWS, COLS)],
        everyone, ens, before, after,
        sems=[pltpu.SemaphoreType.DMA((3,))], away=True,
    )
    advected = moved[:, :LEV].transpose(1, 2, 0).reshape(LEV, 1, FINE_R * FINE_C)
    return (advected, gradient[None])


def solution(mesh):
    member = ("chip", "core")
    tile = ("band", "chip", "core")
    return jax.shard_map(
        shards,
        mesh=jax.sharding.Mesh(mesh.devices.reshape(CHIPS, 2, BANDS), ("chip", "core", "band")),
        in_specs=(
            P(member, None, "band", None),
            P(member, None, "band", None),
            P("band"),
            P("band"),
            P(None, tile, None),
            P(tile, None),
            P(None, tile, None),
            P(tile, None),
        ),
        out_specs=(P(None, tile, None), P(member, None, "band", None)),
        check_vma=False,
    )
```

```python
import functools
import math

import jax
import jax.numpy as jnp
from jax import lax
from jax.experimental import pallas as pl
from jax.experimental.pallas import tpu as pltpu
from jax.sharding import PartitionSpec as P

LEV = 12
LPAD = 16
ROWS = 16
COLS = 512
CHIPS = 32
BANDS = 8
BLOCK = 8
FRAME = BLOCK + 2
FINE_R = 48
FINE_C = 24
NOBS = 256
MAIN = LEV * ROWS
Q = MAIN + 2 * LEV
TILES = 17
CHUNK = TILES * 128
PAIR = CHIPS * TILES

advect_rate = 0.25
highest = lax.Precision.HIGHEST


def lon_smooth(x):
    axis = x.ndim - 1
    return 0.25 * pltpu.roll(x, 1, axis) + 0.5 * x + 0.25 * pltpu.roll(x, COLS - 1, axis)


def interp(j):
    n = 2 * j + 4
    return n // 6, (n % 6) / 6.0


def halo_kernel(alpha_hbm, ens_hbm, last_ref, first_ref, alpha_ref, ens_ref, sems):
    copies = [pltpu.make_async_copy(alpha_hbm, alpha_ref, sems.at[0]), pltpu.make_async_copy(ens_hbm, ens_ref, sems.at[1])]
    for copy in copies:
        copy.start()
    for copy in copies:
        copy.wait()
    last_ref[0] = alpha_ref[:, ROWS - 2, :]
    last_ref[1] = alpha_ref[:, ROWS - 1, :]
    last_ref[2] = ens_ref[:, ROWS - 1, :].astype(jnp.float32)
    first_ref[0] = alpha_ref[:, 0, :]
    first_ref[1] = alpha_ref[:, 1, :]
    first_ref[2] = ens_ref[:, 0, :].astype(jnp.float32)


def product_kernel(scale, spot_ref, alpha_ref, ens_ref, prev_ref, next_ref, sides_ref, keep_ref, send_ref, pad, x_ref, xt_lo, xt_hi, flat):
    pad[:, 8:24, :] = alpha_ref[...]
    pad[:, 7, :] = prev_ref[1]
    pad[:, 24, :] = next_ref[0]
    body = 0.25 * pad[:, 7:23, :] + 0.5 * alpha_ref[...] + 0.25 * pad[:, 9:25, :]
    body = lon_smooth(body) * (ens_ref[...].astype(jnp.float32) * scale)
    top = 0.25 * prev_ref[0] + 0.5 * prev_ref[1] + 0.25 * alpha_ref[:, 0, :]
    low = 0.25 * alpha_ref[:, ROWS - 1, :] + 0.5 * next_ref[0] + 0.25 * next_ref[1]
    x_ref[:MAIN, :] = body.reshape(MAIN, COLS)
    x_ref[MAIN : MAIN + LEV, :] = lon_smooth(top) * (prev_ref[2] * scale)
    x_ref[MAIN + LEV : Q, :] = lon_smooth(low) * (next_ref[2] * scale)
    x_ref[Q:, :] = jnp.zeros((256 - Q, COLS), jnp.float32)
    for half, xt in enumerate((xt_lo, xt_hi)):
        xt[8 : 8 + COLS, :] = x_ref[128 * half : 128 * (half + 1), :].T
        xt[7:8, :] = xt[7 + COLS : 8 + COLS, :]
        xt[8 + COLS : 9 + COLS, :] = xt[8:9, :]
    flat[:, :, FRAME * Q :] = jnp.zeros((2, CHIPS, CHUNK - FRAME * Q), jnp.float32)
    for core in range(2):
        for c in range(FRAME):
            rows = pl.ds(7 + c + BLOCK * core, CHIPS, stride=2 * BLOCK)
            flat[core, :, c * Q : c * Q + 128] = xt_lo[rows, :]
            flat[core, :, c * Q + 128 : (c + 1) * Q] = xt_hi[rows, :][:, : Q - 128]
    first = spot_ref[0:1, :128] == 0.0
    for t in range(TILES):
        even = flat[0, :, 128 * t : 128 * (t + 1)]
        odd = flat[1, :, 128 * t : 128 * (t + 1)]
        keep_ref[pl.ds(t, CHIPS, stride=TILES), :] = jnp.where(first, even, odd)
        send_ref[pl.ds(t, CHIPS, stride=TILES), :] = jnp.where(first, odd, even)
    send_ref[PAIR:, :] = sides_ref[...]


def pair_kernel(spot_ref, keep_ref, both_ref, out_ref, near_ref):
    first = spot_ref[0:1, :128] == 0.0
    out_ref[...] = keep_ref[...] + jnp.where(first, both_ref[PAIR + LPAD : 2 * PAIR + LPAD, :], both_ref[:PAIR, :])
    near_ref[...] = jnp.where(first, both_ref[2 * PAIR + LPAD :, :], both_ref[PAIR : PAIR + LPAD, :])


def split_dot(x, pick, dim):
    total = None
    for _ in range(3):
        part = x.astype(jnp.bfloat16)
        x = x - part.astype(jnp.float32)
        got = lax.dot_general(part, pick, (((1,), (dim,)), ((), ())), preferred_element_type=jnp.float32)
        total = got if total is None else total + got
    return total


def places(lat_ref):
    q = lax.broadcasted_iota(jnp.int32, (1, Q), 1)
    spot = jnp.where(q < MAIN, (q & 15) + 1, jnp.where(q < MAIN + LEV, 0, ROWS + 1))
    level = jnp.where(q < MAIN, q >> 4, jnp.where(q < MAIN + LEV, q - MAIN, q - MAIN - LEV))
    mask = lax.broadcasted_iota(jnp.int32, (LPAD, Q), 0) == level
    low = lat_ref[:, 0:1] + 1.0
    weight = lat_ref[:, 1:2]

    def table(place):
        place = place.astype(jnp.float32)
        return jnp.where(place == low, 1.0 - weight, 0.0) + jnp.where(place == low + 1.0, weight, 0.0)

    return spot, mask, table


def to_coarse(coarse, lat, mask, flat, ref):
    wide = jnp.dot(coarse, lat, precision=highest, preferred_element_type=jnp.float32).reshape(FRAME, LPAD, Q)
    for c in range(FRAME):
        flat[0:1, c * Q : (c + 1) * Q] = jnp.sum(jnp.where(mask, wide[c], 0.0), axis=0, keepdims=True)
    for t in range(TILES):
        ref[t : t + 1, :] = flat[0:1, 128 * t : 128 * (t + 1)]


def own_kernel(coarse_ref, lat_ref, own_ref, flat):
    flat[...] = jnp.zeros_like(flat)
    spot, mask, table = places(lat_ref)
    to_coarse(coarse_ref[...], table(spot), mask, flat, own_ref)


def tile_kernel(spot_ref, g_ref, near_ref, far_ref, bg_ref, lat_ref, obs_ref, adv_ref, coarse_ref, edge_ref, flat):
    for t in range(TILES):
        part = g_ref[pl.ds(t, CHIPS, stride=TILES), :]
        flat[0:1, 128 * t : 128 * (t + 1)] = jnp.sum(part, axis=0, keepdims=True)
    first = spot_ref[0:1, :FINE_R] == 0.0
    near, far = near_ref[:, :FINE_R], far_ref[...]
    ground = [jnp.where(first, far, near)] + [bg_ref[j] for j in range(FINE_C)] + [jnp.where(first, near, far)]
    spot, mask, table = places(lat_ref)
    lat = table(spot)
    spread = [jnp.where(mask, flat[0:1, c * Q : (c + 1) * Q], 0.0) for c in range(FRAME)]
    lat_rows = lax.dot_general(jnp.concatenate(spread, axis=0), lat, (((1,), (1,)), ((), ())), precision=highest,
                               preferred_element_type=jnp.float32).reshape(FRAME, LPAD, FINE_R)
    state = []
    for j in range(-1, FINE_C + 1):
        lo, f = interp(j)
        state.append((1.0 - f) * lat_rows[lo] + f * lat_rows[lo + 1] + ground[j + 1])
    slope = [0.5 * (state[j + 2] - state[j]) for j in range(FINE_C)]
    model = [state[j + 1] - advect_rate * state[j + 1] * slope[j] for j in range(FINE_C)]
    for j in range(FINE_C):
        adv_ref[j] = model[j]
    value = obs_ref[0:LPAD, :]
    precision = obs_ref[LPAD : LPAD + 1, :]
    row = obs_ref[LPAD + 1 : LPAD + 2, :]
    col = obs_ref[LPAD + 2 : LPAD + 3, :]
    fine_row = lax.broadcasted_iota(jnp.int32, (FINE_R, NOBS), 0).astype(jnp.float32)
    pick_row = jnp.where(fine_row == row, 1.0, 0.0).astype(jnp.bfloat16)
    pick_col = [jnp.where(col == float(j), 1.0, 0.0) for j in range(FINE_C)]
    seen = split_dot(jnp.concatenate(model, axis=0), pick_row, 0).reshape(FINE_C, LPAD, NOBS)
    observed = sum(pick_col[j] * seen[j] for j in range(FINE_C))
    weighted = precision * (observed - value)
    back = jnp.concatenate([pick_col[j] * weighted for j in range(FINE_C)], axis=0)
    cot = split_dot(back, pick_row, 1).reshape(FINE_C, LPAD, FINE_R)
    half_rate = 0.5 * advect_rate
    flux = [half_rate * state[j + 1] * cot[j] for j in range(FINE_C)]
    total = [None] * FRAME
    for j in range(-1, FINE_C + 1):
        adj = None
        if 0 <= j < FINE_C:
            adj = cot[j] - advect_rate * cot[j] * slope[j]
        if j + 1 < FINE_C:
            adj = flux[j + 1] if adj is None else adj + flux[j + 1]
        if j - 1 >= 0:
            adj = -flux[j - 1] if adj is None else adj - flux[j - 1]
        lo, f = interp(j)
        for c, w in ((lo, 1.0 - f), (lo + 1, f)):
            if w:
                total[c] = w * adj if total[c] is None else total[c] + w * adj
    coarse = jnp.concatenate(total, axis=0)

    coarse_ref[...] = coarse
    to_coarse(coarse, table(jnp.where(spot < 2, spot + ROWS, spot - ROWS)), mask, flat, edge_ref)


def share_kernel(spot_ref, own_ref, one_ref, two_ref, out_ref):
    even = spot_ref[1:2, :128] == 0.0
    before = jnp.where(even, two_ref[...], one_ref[...])
    after = jnp.where(even, one_ref[...], two_ref[...])
    shape = (TILES, 128)
    q = lax.rem(lax.broadcasted_iota(jnp.int32, shape, 0) * 128 + lax.broadcasted_iota(jnp.int32, shape, 1), Q)
    row = q & 15
    inner = q < MAIN
    from_prev = (inner & (row == 0)) | ((q >= MAIN) & (q < MAIN + LEV))
    from_next = (inner & (row == ROWS - 1)) | (q >= MAIN + LEV)
    total = own_ref[...] + jnp.where(from_prev, before, 0.0) + jnp.where(from_next, after, 0.0)
    for m in range(CHIPS):
        out_ref[TILES * m : TILES * (m + 1), :] = total


def gradient_kernel(scale, g_ref, ens_ref, prev_ref, next_ref, out_hbm, pad, xt_lo, xt_hi, flat, out_ref, sems):
    for core in range(2):
        for t in range(TILES):
            flat[core, :, 128 * t : 128 * (t + 1)] = g_ref[pl.ds(core * CHIPS * TILES + t, CHIPS, stride=TILES), :]
    slots = [[flat[core, :, c * Q : (c + 1) * Q] for c in range(FRAME)] for core in range(2)]
    even, odd = slots
    even_first = even[1] + pltpu.roll(odd[FRAME - 1], 1, 0)
    even_last = even[BLOCK] + odd[0]
    odd_first = odd[1] + even[FRAME - 1]
    odd_last = odd[BLOCK] + pltpu.roll(even[0], CHIPS - 1, 0)
    even[1], even[BLOCK], odd[1], odd[BLOCK] = even_first, even_last, odd_first, odd_last
    for core in range(2):
        for c in range(1, BLOCK + 1):
            rows = pl.ds(c - 1 + BLOCK * core, CHIPS, stride=2 * BLOCK)
            xt_lo[rows, :] = slots[core][c][:, :128]
            xt_hi[rows, : Q - 128] = slots[core][c][:, 128:]
    lo = xt_lo[...].T * scale
    hi = xt_hi[...].T * scale
    field = jnp.concatenate([lo, hi[: MAIN - 128, :]], axis=0).reshape(LEV, ROWS, COLS) * ens_ref[...].astype(jnp.float32)
    pad[:, 8:24, :] = field
    pad[:, 7, :] = hi[MAIN - 128 : MAIN - 128 + LEV, :] * prev_ref[2]
    pad[:, 24, :] = hi[MAIN - 128 + LEV : Q - 128, :] * next_ref[2]
    copies = []
    for k in range(3):
        lev = slice(4 * k, 4 * (k + 1))
        out_ref[lev] = lon_smooth(0.25 * pad[lev, 7:23, :] + 0.5 * pad[lev, 8:24, :] + 0.25 * pad[lev, 9:25, :])
        copies.append(pltpu.make_async_copy(out_ref.at[lev], out_hbm.at[lev], sems.at[k]))
        copies[k].start()
    for copy in copies:
        copy.wait()


def call(kernel, out, scratch, *args, hbm=False, sems=(), away=False):
    def spec(x):
        return pl.BlockSpec(memory_space=pltpu.SMEM if x.dtype == jnp.int32 else pltpu.VMEM)

    return pl.pallas_call(
        kernel,
        out_shape=out,
        in_specs=[pl.BlockSpec(memory_space=pltpu.HBM) if hbm else spec(x) for x in args],
        out_specs=pl.BlockSpec(memory_space=pl.ANY) if away else jax.tree.map(spec, out),
        scratch_shapes=[pltpu.VMEM(shape, jnp.float32) for shape in scratch] + list(sems),
        compiler_params=pltpu.CompilerParams(vmem_limit_bytes=40 * 1024 * 1024),
    )(*args)


def f32(*shape):
    return jax.ShapeDtypeStruct(shape, jnp.float32)


def both_ways(up_value, down_value, axis, size, wrap):
    up = [(i, (i + 1) % size) for i in range(size if wrap else size - 1)]
    down = [(j, i) for i, j in up]
    return lax.ppermute(up_value, axis, up), lax.ppermute(down_value, axis, down)


def exchange(flat, tiles):
    parts = lax.all_to_all(flat.reshape(CHIPS, 1, tiles * 128), "chip", 0, 0, tiled=True)
    return parts.reshape(CHIPS * tiles, 128)


def shards(ensemble, alpha, lat_lower, lat_weight, background, obs_cell, obs_value, obs_precision):
    scale = 1.0 / math.sqrt(2 * CHIPS - 1)
    spot = jnp.stack([lax.axis_index("core"), lax.axis_index("band") % 2]).astype(jnp.float32)
    spot = jnp.broadcast_to(spot[:, None], (2, COLS))
    last, first, alf, ens = call(
        halo_kernel,
        (f32(3, LEV, COLS), f32(3, LEV, COLS), f32(LEV, ROWS, COLS), jax.ShapeDtypeStruct((LEV, ROWS, COLS), jnp.bfloat16)),
        [], pltpu.with_memory_space_constraint(alpha[0], pltpu.HBM), pltpu.with_memory_space_constraint(ensemble[0], pltpu.HBM), hbm=True, sems=[pltpu.SemaphoreType.DMA((2,))],
    )
    before, after = both_ways(last, first, "band", BANDS, False)

    grid = background.reshape(LEV, FINE_R, FINE_C).transpose(2, 0, 1)
    first_core = lax.axis_index("core") == 0
    sides = jnp.where(first_core, grid[FINE_C - 1], grid[0])
    sides = jnp.pad(sides, ((0, LPAD - LEV), (0, 128 - FINE_R)))
    far = jnp.where(first_core, grid[0], grid[FINE_C - 1])
    size = 2 * CHIPS
    ground = jnp.pad(grid, ((0, 0), (0, LPAD - LEV), (0, 0)))
    obs = jnp.concatenate(
        [jnp.pad(obs_value[:, 0, :], ((0, LPAD - LEV), (0, 0))), obs_precision, (obs_cell // FINE_C).astype(jnp.float32),
         (obs_cell % FINE_C).astype(jnp.float32), jnp.zeros((24 - LPAD - 3, NOBS), jnp.float32)], axis=0)
    lat = jnp.stack([lat_lower.astype(jnp.float32), lat_weight], axis=1)
    before, after, ground, sides, far = lax.optimization_barrier((before, after, ground, sides, far))

    keep, send = call(
        functools.partial(product_kernel, scale),
        (f32(PAIR, 128), f32(PAIR + LPAD, 128)),
        [(LEV, 32, COLS), (256, COLS), (COLS + 16, 128), (COLS + 16, 128), (2, CHIPS, CHUNK)],
        spot, alf, ens, before, after, sides,
    )
    both = lax.all_gather(send, "core", axis=0, tiled=True)
    paired, near = call(pair_kernel, (f32(PAIR, 128), f32(LPAD, 128)), [], spot, keep, both)
    paired, far = lax.optimization_barrier((paired, far))
    gathered = exchange(paired, TILES)
    far = lax.ppermute(far, ("chip", "core"), [(i, (i + (1 if i % 2 else size - 1)) % size) for i in range(size)])
    far = jnp.pad(far, ((0, LPAD - LEV), (0, 0)))
    moved, coarse, edge = call(
        tile_kernel,
        (f32(FINE_C, LPAD, FINE_R), f32(FRAME * LPAD, FINE_R), f32(TILES, 128)),
        [(8, CHUNK)],
        spot, gathered, near, far, ground, lat, obs,
    )
    one = lax.ppermute(edge, "band", [(b, b ^ 1) for b in range(BANDS)])
    two = lax.ppermute(edge, "band", [(b, ((b + 1) ^ 1) - 1) for b in range(1, BANDS - 1)])
    own = call(own_kernel, f32(TILES, 128), [(8, CHUNK)], coarse, lat)
    shared = call(share_kernel, f32(CHIPS * TILES, 128), [], spot, own, one, two)
    everyone = lax.all_gather(exchange(shared, TILES), "core", axis=0, tiled=True)
    gradient = call(
        functools.partial(gradient_kernel, scale),
        f32(LEV, ROWS, COLS),
        [(LEV, 32, COLS), (COLS, 128), (COLS, 128), (2, CHIPS, CHUNK), (LEV, ROWS, COLS)],
        everyone, ens, before, after,
        sems=[pltpu.SemaphoreType.DMA((3,))], away=True,
    )
    advected = moved[:, :LEV].transpose(1, 2, 0).reshape(LEV, 1, FINE_R * FINE_C)
    return (advected, gradient[None])


def solution(mesh):
    member = ("chip", "core")
    tile = ("band", "chip", "core")
    return jax.shard_map(
        shards,
        mesh=jax.sharding.Mesh(mesh.devices.reshape(CHIPS, 2, BANDS), ("chip", "core", "band")),
        in_specs=(
            P(member, None, "band", None),
            P(member, None, "band", None),
            P("band"),
            P("band"),
            P(None, tile, None),
            P(tile, None),
            P(None, tile, None),
            P(tile, None),
        ),
        out_specs=(P(None, tile, None), P(member, None, "band", None)),
        check_vma=False,
    )
```
